32 devices in a mesh: row: 8 (over z, y), col: 4 (over x, core).
Axes of the slice: x: 2, y: 2, z: 4, core: 2. Of those that a mesh axis runs over, the one named last changes fastest.
Arguments:
- three_centre: bfloat16 [192, 512, 512], P('row', 'col'), may hold values from -0.25 to 0.25
- tensor_pattern: int32 [192, 4, 4], P('row'), may hold values 0 or 1
- occ_density: bfloat16 [512, 512], P('row'), may hold values from -0.25 to 0.25
- virt_density: bfloat16 [512, 512], P('row'), may hold values from -0.25 to 0.25
- density_pattern: int32 [4, 4], replicated, may hold values 0 or 1
Outputs:
- response: float32 [192, 192], P('row')
The draws below stay inside these ranges and needn't reach their ends.
All inputs are finite; a program needn't handle non-finite values. No bound on the sum of `tensor_pattern` on one device may be relied on, other than what follows from the above.
Results may differ from the reference program's by a relative error of at most 0.0041.
Values may be sent and summed in bfloat16 or wider, within the bound.
A program may use at most 64 MiB of HBM per device.

```python
import jax
import jax.numpy as jnp
from jax import lax

BS = 128
NBLK = 4
NAO = 512
NAUX = 192


def with_ends(values, stream_key, smallest, largest):
    longest = values.shape.index(max(values.shape))
    spots = []
    for shift in (0, 1):
        where = [jax.random.randint(jax.random.fold_in(stream_key, axis), (), 0, length) for axis, length in enumerate(values.shape)]
        where[longest] = (where[longest] + shift) % values.shape[longest]
        spots.append(tuple(where))
    return values.at[spots[0]].set(smallest).at[spots[1]].set(largest)


def level_of(own_key, shape, shards, smallest, high):
    def one(dim, parts):
        draws = jax.random.uniform(jax.random.fold_in(jax.random.fold_in(own_key, 6), dim), (parts,), jnp.float32, smallest / len(shards), high / len(shards))
        return jnp.repeat(jnp.exp(draws), shape[dim] // parts).reshape((-1,) + (1,) * (len(shape) - dim - 1))

    factor_of = one(*shards[0])
    for cut in shards[1:]:
        factor_of = factor_of * one(*cut)
    return factor_of


def gaussian(rng, extent, width, reach, shards=(), kind=jnp.bfloat16):
    entries = jax.random.normal(rng, extent, jnp.float32) * width
    if len(shards) > 0:
        entries = level_of(rng, extent, shards, -0.22, 0.18) * entries
    return jnp.clip(entries, min=-reach, max=reach).astype(kind)


def setup_inputs(seed: int = 0) -> dict:
    arg_keys = jax.random.split(jax.random.key(seed), 6)
    return {
        "three_centre": gaussian(arg_keys[0], (NAUX, NAO, NAO), NAO ** -0.5, 0.25, ((0, 8), (1, 4))),
        "tensor_pattern": with_ends((jax.random.randint(arg_keys[1], (NAUX, NBLK, NBLK), 0, 4) < 3).astype(jnp.int32), jax.random.fold_in(arg_keys[1], 1), 0, 1),
        "occ_density": gaussian(arg_keys[2], (NAO, NAO), NAO ** -0.5, 0.25, ((0, 8),)),
        "virt_density": gaussian(arg_keys[3], (NAO, NAO), NAO ** -0.5, 0.25, ((0, 8),)),
        "density_pattern": with_ends((jax.random.randint(arg_keys[4], (NBLK, NBLK), 0, 4) < 3).astype(jnp.int32), jax.random.fold_in(arg_keys[4], 1), 0, 1),
    }


def expand_blocks(pattern, block_size, first, second):
    return jnp.repeat(jnp.repeat(pattern, block_size, first), block_size, second)


def reference(three_centre, tensor_pattern, occ_density, virt_density, density_pattern):
    density_mask = expand_blocks(density_pattern, BS, 0, 1).astype(occ_density.dtype)
    occupied = occ_density * density_mask
    virtual = virt_density * density_mask

    def per_aux(items):
        tensor_row, pattern_row = items
        masked = tensor_row * expand_blocks(pattern_row, BS, 0, 1).astype(tensor_row.dtype)
        moved = jnp.dot(masked, virtual, preferred_element_type=jnp.float32).astype(jnp.bfloat16)
        second = jnp.dot(occupied, moved, preferred_element_type=jnp.float32).astype(jnp.bfloat16)
        return second, masked

    second_all, masked_all = lax.map(per_aux, (three_centre, tensor_pattern))
    left_flat = second_all.reshape(NAUX, NAO * NAO)
    right_flat = masked_all.reshape(NAUX, NAO * NAO)
    return lax.dot_general(left_flat, right_flat, (((1,), (1,)), ((), ())), preferred_element_type=jnp.float32)
```

```python
import functools

import jax
import jax.numpy as jnp
from jax import lax
from jax.experimental import pallas as pl
from jax.experimental.pallas import tpu as pltpu
from jax.sharding import PartitionSpec as P

BS = 128
MESH = pl.DeviceIdType.MESH


def expand_blocks(pattern, block_size, first, second):
    return jnp.repeat(jnp.repeat(pattern, block_size, first), block_size, second)


def partner(me, k, count):
    if count & (count - 1):
        return lax.rem(me + k, count), lax.rem(me + count - k, count)
    bit, other = 1, me
    while bit < count:
        if k & bit:
            other = other + bit - 2 * bit * ((me // bit) % 2)
        bit *= 2
    return other, other


def near_first(count):
    half = [k for k in range(2, count // 2)]
    return half + [1] * (count > 1) + [k for k in range(max(2, count // 2), count)]


def greet(me_row, me_col, rows, cols):
    barrier = pltpu.get_barrier_semaphore()
    for i in range(rows):
        for j in range(cols):
            if i or j:
                pl.semaphore_signal(
                    barrier,
                    inc=1,
                    device_id=(lax.rem(me_row + i, rows), lax.rem(me_col + j, cols)),
                    device_id_type=MESH,
                )
    pl.semaphore_wait(barrier, rows * cols - 1)


def exchange_kernel(
    rows, cols, chunks,
    tensor_ref, pattern_ref, occ_ref, virt_ref, density_ref,
    out_ref,
    b_in, s_in, b_lines, wide_rows, part, landed, total, others,
    masked, virt_all, occ_all, moved, moved_cols, second,
    gather_send, gather_recv, spread_send, spread_recv,
    b_send, b_recv, m_send, m_recv, s_send, s_recv, own_sem, load_sem, row_send, row_recv, col_send, col_recv,
):
    me_row, me_col = lax.axis_index("row"), lax.axis_index("col")
    aux, local, orb = tensor_ref.shape
    strip = local // rows
    wide = orb // cols
    blocks = orb // BS
    quarter = virt_ref.shape[0] // cols
    row_steps = near_first(rows)

    def remote(src, dst, send, recv, to_row, to_col):
        copy = pltpu.make_async_remote_copy(
            src_ref=src, dst_ref=dst, send_sem=send, recv_sem=recv,
            device_id=(to_row, to_col), device_id_type=MESH,
        )
        copy.start()
        return copy

    load = pltpu.make_async_copy(tensor_ref, masked, load_sem)
    load.start()
    greet(me_row, me_col, rows, cols)

    share = pl.ds(pl.multiple_of(me_col * quarter, quarter), quarter)
    gathers = []
    owns = []
    for d, (src, dst) in enumerate(((virt_ref, virt_all), (occ_ref, occ_all))):
        own = pltpu.make_async_copy(src.at[share], dst.at[me_row, me_col], own_sem.at[d])
        own.start()
        owns.append(own)
        gathers.append([
            remote(src.at[share], dst.at[me_row, me_col],
                   gather_send.at[d, k], gather_recv.at[d, k],
                   partner(me_row, k, rows)[0], me_col)
            for k in row_steps
        ])

    block_row = (me_col * local) // BS

    def mask_one(p, carry):
        for j in range(blocks):
            keep = pattern_ref[block_row, j, p].astype(jnp.float32)
            piece = masked[p, :, j * BS:(j + 1) * BS].astype(jnp.float32)
            masked[p, :, j * BS:(j + 1) * BS] = (piece * keep).astype(jnp.bfloat16)
        return carry

    load.wait()
    lax.fori_loop(0, aux, mask_one, 0)

    b_copies = []
    for k in row_steps:
        to_row = partner(me_row, k, rows)[0]
        theirs = pl.ds(pl.multiple_of(to_row * strip, strip), strip)
        b_copies.append(remote(masked.at[:, theirs, :], b_in.at[me_row],
                               b_send.at[k], b_recv.at[k], to_row, me_col))
    own_part = pl.ds(pl.multiple_of(me_row * strip, strip), strip)
    own_b = pltpu.make_async_copy(masked.at[:, own_part, :], b_in.at[me_row], own_sem.at[2])
    own_b.start()

    spreads = []
    for d, full in enumerate((virt_all, occ_all)):
        owns[d].wait()
        for copy in gathers[d]:
            copy.wait_recv()
        spreads.append([
            remote(full.at[:, me_col], full.at[:, me_col],
                   spread_send.at[d, k], spread_recv.at[d, k],
                   me_row, partner(me_col, k, cols)[0])
            for k in range(1, cols)
        ])

    def take_density(full, d):
        for copy in spreads[d]:
            copy.wait()
        for copy in gathers[d]:
            copy.wait_send()
        values = full[...].reshape(orb, orb)
        lines = []
        for i in range(blocks):
            line = []
            for j in range(blocks):
                keep = density_ref[i, j].astype(jnp.float32)
                piece = values[i * BS:(i + 1) * BS, j * BS:(j + 1) * BS].astype(jnp.float32)
                line.append((piece * keep).astype(jnp.bfloat16))
            lines.append(jnp.concatenate(line, axis=1))
        full[...] = jnp.concatenate(lines, axis=0).reshape(full.shape)

    take_density(virt_all, 0)

    def move_one(p, carry):
        product = jnp.dot(masked[p], virt_all[...].reshape(orb, orb),
                          preferred_element_type=jnp.float32).astype(jnp.bfloat16)
        for j in range(cols):
            moved[j, p] = product[:, j * wide:(j + 1) * wide]
        return carry

    span = aux // chunks
    m_copies = []
    for h in range(chunks):
        lax.fori_loop(h * span, (h + 1) * span, move_one, 0)
        piece = pl.ds(h * span, span)
        copies = []
        for k in range(1, cols):
            to_col = partner(me_col, k, cols)[0]
            copies.append(remote(moved.at[to_col, piece], moved_cols.at[me_col, piece],
                                 m_send.at[h, k], m_recv.at[h, k], me_row, to_col))
        own = pltpu.make_async_copy(moved.at[me_col, piece], moved_cols.at[me_col, piece],
                                    own_sem.at[5 + h])
        own.start()
        m_copies.append(copies + [own])

    take_density(occ_all, 1)

    def second_two(p, carry):
        rhs = jnp.concatenate(
            [moved_cols[:, 2 * p + h].reshape(orb, wide) for h in range(2)], axis=1)
        product = jnp.dot(occ_all[...].reshape(orb, orb), rhs,
                          preferred_element_type=jnp.float32).astype(jnp.bfloat16)
        for h in range(2):
            second[2 * p + h] = product[:, h * wide:(h + 1) * wide]
        return carry

    lanes = pl.ds(pl.multiple_of(me_col * wide, wide), wide)

    def strip_of(to_row, to_col):
        return pl.ds(pl.multiple_of(to_col * local + to_row * strip, strip), strip)

    s_copies = [[] for _ in range(chunks)]
    for h in range(chunks):
        piece = pl.ds(h * span, span)
        for copy in m_copies[h]:
            copy.wait()
        lax.fori_loop(h * span // 2, (h + 1) * span // 2, second_two, 0)
        for k in [0] + row_steps:
            for q in range(cols):
                if k or q:
                    to_row, to_col = partner(me_row, k, rows)[0], partner(me_col, q, cols)[0]
                    s_copies[h].append(remote(
                        second.at[piece, strip_of(to_row, to_col), :],
                        s_in.at[me_row, piece, :, lanes],
                        s_send.at[h, k, q], s_recv.at[h, k, q], to_row, to_col))
    own_s = pltpu.make_async_copy(second.at[:, strip_of(me_row, me_col), :],
                                  s_in.at[me_row, :, :, lanes], own_sem.at[4])
    own_s.start()

    def widen(p, carry):
        rows_at = pl.ds(pl.multiple_of(p * aux * strip, aux * strip), aux * strip)
        for j in range(orb // BS):
            wide_rows[j, rows_at, :] = b_in[p, :, :, j * BS:(j + 1) * BS].reshape(
                aux * strip, BS).astype(jnp.float32)
        return carry

    def every(line, count):
        return jnp.concatenate(
            [wide_rows[j, pl.ds(line, count, stride=strip), :] for j in range(orb // BS)],
            axis=1).astype(jnp.bfloat16)

    own_b.wait()
    for copy in b_copies:
        copy.wait()
    lax.fori_loop(0, rows, widen, 0)
    for line in range(strip):
        b_lines[line] = every(line, rows * aux)

    own_s.wait()
    for h in range(chunks):
        for copy in s_copies[h]:
            copy.wait()
        count = rows * span
        for j in range(orb // BS):
            wide_rows[j, 0:count * strip, :] = s_in[
                :, h * span:(h + 1) * span, :, j * BS:(j + 1) * BS].reshape(
                count * strip, BS).astype(jnp.float32)
        chi = jnp.zeros((count, rows * aux), jnp.float32)
        for line in range(strip):
            chi = chi + lax.dot_general(every(line, count), b_lines[line], (((1,), (1,)), ((), ())),
                                        preferred_element_type=jnp.float32)
        part[:, h * span:(h + 1) * span, :] = chi.reshape(rows, span, rows * aux)

    copies = []
    for k in row_steps:
        to_row = partner(me_row, k, rows)[0]
        copies.append(remote(part.at[to_row], landed.at[k],
                             row_send.at[k], row_recv.at[k], to_row, me_col))
    value = part[me_row]
    for copy in copies:
        copy.wait()
    for k in range(1, rows):
        value = value + landed[k]
    total[...] = value
    copies = []
    for k in range(1, cols):
        to_col = partner(me_col, k, cols)[0]
        copies.append(remote(total, others.at[me_col],
                             col_send.at[k], col_recv.at[k], me_row, to_col))
    others[me_col] = value
    for copy in copies:
        copy.wait()
    value = others[0]
    for k in range(1, cols):
        value = value + others[k]
    out_ref[...] = value


def direct(rows, cols, three_centre, tensor_pattern, occ_density, virt_density, density_pattern):
    aux, local, orb = three_centre.shape
    strip, wide = local // rows, orb // cols
    quarter = occ_density.shape[0] // cols
    bf16 = jnp.bfloat16
    chunks = aux // 8
    total = rows * aux
    f32 = jnp.float32
    dma = pltpu.SemaphoreType.DMA
    vmem = pl.BlockSpec(memory_space=pltpu.VMEM)
    smem = pl.BlockSpec(memory_space=pltpu.SMEM)
    hbm = pl.BlockSpec(memory_space=pltpu.MemorySpace.HBM)
    return pl.pallas_call(
        functools.partial(exchange_kernel, rows, cols, chunks),
        out_shape=jax.ShapeDtypeStruct((aux, total), f32),
        in_specs=[hbm, smem, hbm, hbm, smem],
        out_specs=vmem,
        scratch_shapes=[
            pltpu.VMEM((rows, aux, strip, orb), bf16),
            pltpu.VMEM((rows, aux, strip, orb), bf16),
            pltpu.VMEM((strip, total, orb), bf16),
            pltpu.VMEM((orb // BS, total * strip, BS), f32),
            pltpu.VMEM((rows, aux, total), f32),
            pltpu.VMEM((rows, aux, total), f32),
            pltpu.VMEM((aux, total), f32),
            pltpu.VMEM((cols, aux, total), f32),
            pltpu.VMEM((aux, local, orb), bf16),
            pltpu.VMEM((rows, cols, quarter, orb), bf16),
            pltpu.VMEM((rows, cols, quarter, orb), bf16),
            pltpu.VMEM((cols, aux, local, wide), bf16),
            pltpu.VMEM((cols, aux, local, wide), bf16),
            pltpu.VMEM((aux, orb, wide), bf16),
            dma((2, rows)), dma((2, rows)), dma((2, cols)), dma((2, cols)),
            dma((rows,)), dma((rows,)), dma((chunks, cols)), dma((chunks, cols)),
            dma((chunks, rows, cols)), dma((chunks, rows, cols)), dma((5 + chunks,)), dma(()),
            dma((rows,)), dma((rows,)), dma((cols,)), dma((cols,)),
        ],
        compiler_params=pltpu.CompilerParams(
            collective_id=0, has_side_effects=True, vmem_limit_bytes=67_000_000),
    )(three_centre, tensor_pattern.transpose(1, 2, 0), occ_density, virt_density,
      density_pattern)


def layered_kernel(
    rows, cols, chunks,
    tensor_ref, pattern_ref, occ_ref, virt_ref, density_ref,
    out_ref,
    whole, layer, stage, hub, wide_rows, direct_sum, swapped_sum, part, landed, total, others,
    virt_all, occ_all, right, lefts,
    load_sem, own_sem, gather_send, gather_recv, spread_send, spread_recv,
    cut_send, cut_recv, x_send, x_recv, y_send, y_recv, z_send, z_recv,
    pass_send, row_send, row_recv, col_send, col_recv,
):
    me_row, me_col = lax.axis_index("row"), lax.axis_index("col")
    z, y = me_row // 2, me_row % 2
    x, core = me_col // 2, me_col % 2
    aux, local, orb = tensor_ref.shape
    unit = local // 8
    half = orb // 2
    blocks = orb // BS
    span = aux // chunks
    share_rows = virt_ref.shape[0] // 2
    row_steps = near_first(rows)
    bf16, f32 = jnp.bfloat16, jnp.float32
    X, S, T = 0, 1, 2
    mate_col, across_col = 2 * x + 1 - core, 2 * (1 - x) + core
    diagonal_col = 2 * (1 - x) + 1 - core
    over_row = 2 * z + 1 - y

    def remote(src, dst, send, recv, to_row, to_col):
        return pltpu.make_async_remote_copy(
            src_ref=src, dst_ref=dst, send_sem=send, recv_sem=recv,
            device_id=(to_row, to_col), device_id_type=MESH,
        )

    def of(h):
        return pl.ds(pl.multiple_of(h * span, span), span)

    def lanes(c):
        return pl.ds(pl.multiple_of(c * half, half), half)

    def load(h):
        return pltpu.make_async_copy(tensor_ref.at[of(h)], whole.at[of(h), me_col], load_sem.at[h])

    def each(count, body):
        def step(i, carry):
            body(i)
            return carry
        lax.fori_loop(0, count, step, 0)

    each(chunks, lambda h: load(h).start())
    barrier = pltpu.get_barrier_semaphore()
    met = [(lax.rem(me_row + i, rows), me_col) for i in range(1, rows)]
    met += [(me_row, lax.rem(me_col + j, cols)) for j in range(1, cols)] + [(over_row, mate_col)]
    for device in met:
        pl.semaphore_signal(barrier, inc=1, device_id=device, device_id_type=MESH)
    pl.semaphore_wait(barrier, len(met))

    share = pl.ds(pl.multiple_of(core * share_rows, share_rows), share_rows)
    gathers, owns = [], []
    for d, (src, dst) in enumerate(((virt_ref, virt_all), (occ_ref, occ_all))):
        own = pltpu.make_async_copy(src.at[share], dst.at[me_row, core], own_sem.at[d])
        own.start()
        owns.append(own)
        copies = [
            remote(src.at[share], dst.at[me_row, core],
                   gather_send.at[d, k], gather_recv.at[d, k],
                   partner(me_row, k, rows)[0], me_col)
            for k in row_steps
        ]
        for copy in copies:
            copy.start()
        gathers.append(copies)

    block_row = (me_col * local) // BS

    def keep(h):
        return pltpu.make_async_copy(
            whole.at[of(h), me_col, :, lanes(core)], layer.at[X, y, of(h)], own_sem.at[2 + h])

    def to_mate(h):
        return remote(whole.at[of(h), me_col, :, lanes(1 - core)], layer.at[X, y, of(h)],
                      cut_send.at[0, h], cut_recv.at[0, h], me_row, mate_col)

    def over(h, c):
        return remote(whole.at[of(h), me_col, :, c * half:(c + 1) * half], layer.at[X, y, of(h)],
                      cut_send.at[c, h], cut_recv.at[1, h], over_row, 2 * x + c)

    def gather_x(h, which):
        block = across_col if which == 2 else me_col
        to_col = across_col if which == 1 else mate_col
        piece = whole.at[of(h), block]
        return remote(piece, piece, x_send.at[which, h], x_recv.at[which, h], me_row, to_col)

    def first(h):
        load(h).wait()

        def mask_one(i):
            p = h * span + i
            for j in range(blocks):
                kept = pattern_ref[block_row, j, p].astype(f32)
                piece = whole[p, me_col, :, j * BS:(j + 1) * BS].astype(f32)
                whole[p, me_col, :, j * BS:(j + 1) * BS] = (piece * kept).astype(bf16)

        each(span, mask_one)

        @pl.when(y == core)
        def _():
            keep(h).start()
            to_mate(h).start()

        @pl.when(y != core)
        def _():
            over(h, 0).start()
            over(h, 1).start()

        gather_x(h, 1).start()
        gather_x(h, 0).start()

    each(chunks, first)

    sends = {
        0: [(X, 2, 0, 0, 6), (X, 1, 0, 5, 3), (S, 1, 1, 5, 3)],
        1: [(X, 2, 1, 0, 6), (X, 0, 0, 0, 5), (S, 0, 1, 0, 5)],
        2: [(X, 3, 2, 3, 5), (S, 1, 2, 6, 2), (T, 1, 4, 6, 2)],
        3: [(S, 2, 2, 0, 3), (S, 1, 3, 6, 2), (T, 2, 3, 0, 3), (T, 1, 5, 6, 2)],
    }
    passed = [(0, 3, 0, 3, 3), (1, 3, 1, 3, 3)]
    lands = {w: sorted([(e[2], e[4]) for v in sends.values() for e in v if e[1] == w]) for w in range(4)}
    lands[3] = sorted(lands[3] + [(e[2], e[4]) for e in passed])

    def slot(k):
        return y if k == 0 else 1 - y

    def z_copy(i, entry, k, h):
        array, to, at, start, count = entry
        return remote(
            layer.at[array, slot(k), of(h), start * unit:(start + count) * unit],
            hub.at[at, slot(k), of(h), 0:count * unit],
            z_send.at[i, k, h], z_recv.at[at, k, h], 2 * to + y, me_col)

    def pass_copy(i, entry, k, h):
        source, to, at, start, count = entry
        return remote(
            hub.at[source, slot(k), of(h), start * unit:(start + count) * unit],
            hub.at[at, slot(k), of(h), 0:count * unit],
            pass_send.at[i, k, h], z_recv.at[at, k, h], 2 * to + y, me_col)

    def landing(at, count, k, h):
        piece = hub.at[at, slot(k), of(h), 0:count * unit]
        return remote(piece, piece, z_send.at[0, k, h], z_recv.at[at, k, h], over_row, me_col)

    def send_z(arrays, k, h):
        for w in range(4):
            mine = [(i, e) for i, e in enumerate(sends[w]) if e[0] in arrays]
            if mine:
                @pl.when(z == w)
                def _():
                    for i, entry in mine:
                        z_copy(i, entry, k, h).start()

    def cut_in(h):
        @pl.when(y == core)
        def _():
            keep(h).wait()

        @pl.when(y != core)
        def _():
            to_mate(h).wait_recv()
        send_z((X,), 0, h)

    each(chunks, cut_in)

    spreads = []
    for d, full in enumerate((virt_all, occ_all)):
        owns[d].wait()
        for copy in gathers[d]:
            copy.wait_recv()
        copies = [
            remote(full.at[:, core], full.at[:, core],
                   spread_send.at[d], spread_recv.at[d], me_row, mate_col)
        ]
        for copy in copies:
            copy.start()
        spreads.append(copies)

    def take_density(full, d):
        for copy in spreads[d]:
            copy.wait()
        for copy in gathers[d]:
            copy.wait_send()
        values = full[...].reshape(orb, orb)
        lines = []
        for i in range(blocks):
            line = []
            for j in range(blocks):
                kept = density_ref[i, j].astype(f32)
                piece = values[i * BS:(i + 1) * BS, j * BS:(j + 1) * BS].astype(f32)
                line.append((piece * kept).astype(bf16))
            lines.append(jnp.concatenate(line, axis=1))
        full[...] = jnp.concatenate(lines, axis=0).reshape(full.shape)

    take_density(virt_all, 0)
    take_density(occ_all, 1)

    for c in range(2):
        @pl.when(core == c)
        def _():
            values = virt_all[...].reshape(orb, orb)
            right[0] = values[:, c * half:(c + 1) * half]
            right[1] = values[c * half:(c + 1) * half, :].astype(f32).T.astype(bf16)

    per = local // (share_rows * 2)
    for k in range(2):
        block = 2 * x + slot(k)
        lefts[0, k * local:(k + 1) * local] = occ_all[pl.ds(block * per, per)].reshape(local, orb)
        for b in range(orb // local):
            @pl.when(block == b)
            def _():
                values = occ_all[...].reshape(orb, orb)
                lefts[1, k * local:(k + 1) * local] = (
                    values[:, b * local:(b + 1) * local].astype(f32).T.astype(bf16))

    def y_copy(d, h):
        return remote(stage.at[d, of(h)], layer.at[S + d, y, of(h)],
                      y_send.at[d, h], y_recv.at[d, h], over_row, me_col)

    def transform(d, p):
        moved = jnp.dot(whole[p].reshape(orb, orb), right[d],
                        preferred_element_type=f32).astype(bf16)
        second = jnp.dot(lefts[d], moved, preferred_element_type=f32).astype(bf16)
        layer[S + d, y, p] = second[:local]
        stage[d, p] = second[local:]

    def late(h):
        y_copy(0, h).wait_recv()

        @pl.when(z >= 2)
        def _():
            y_copy(1, h).wait_recv()
        send_z((S, T), 1, h)

    def hand_on(k, h):
        @pl.when(z == 2)
        def _():
            for i, entry in enumerate(passed):
                landing(entry[0], 6, k, h).wait_recv()
                pass_copy(i, entry, k, h).start()

    lag = chunks // 2

    def main(h):
        gather_x(h, 1).wait_recv()
        gather_x(h, 2).start()
        gather_x(h, 0).wait_recv()
        gather_x(h, 2).wait_recv()

        def one(i):
            p = h * span + i
            transform(0, p)

            @pl.when(z >= 2)
            def _():
                transform(1, p)

        each(span, one)
        y_copy(0, h).start()

        @pl.when(z >= 2)
        def _():
            y_copy(1, h).start()
        send_z((S, T), 0, h)
        over(h, 0).wait_recv()
        send_z((X,), 1, h)

        @pl.when(h >= lag)
        def _():
            late(h - lag)

        @pl.when(h >= 2)
        def _():
            hand_on(0, h - 2)

    each(chunks, main)

    def after(i):
        hand_on(1, i)

        @pl.when(i < 2)
        def _():
            hand_on(0, chunks - 2 + i)

        @pl.when(i % 2 == 1)
        def _():
            late(chunks - lag + i // 2)

    each(chunks, after)

    def settle(h):
        for w in range(4):
            @pl.when(z == w)
            def _():
                for at, count in lands[w]:
                    if w != 2 or at > 1:
                        for k in range(2):
                            landing(at, count, k, h).wait_recv()

    each(chunks, settle)

    direct_sum[...] = jnp.zeros_like(direct_sum)
    swapped_sum[...] = jnp.zeros_like(swapped_sum)
    deep = 2 * aux

    def stretch(start, stop, left, rights):
        def strip(i):
            base = (start + i) * unit
            for n, (ref, shift) in enumerate([e[2:] for e in left] + [e[1:] for e in rights]):
                at = pl.ds(pl.multiple_of(base - shift * unit, unit), unit)
                for j in range(half // BS):
                    wide_rows[n, j] = ref[:, :, at, j * BS:(j + 1) * BS].astype(f32).reshape(
                        deep * unit, BS)

            def every(n, line):
                return jnp.concatenate(
                    [wide_rows[n, j, pl.ds(line, deep, stride=unit), :] for j in range(half // BS)],
                    axis=1).astype(bf16)

            chi = jnp.zeros((deep * len(left), 4 * deep), f32)
            for line in range(unit):
                lhs = jnp.concatenate([every(n, line) for n in range(len(left))], axis=0)
                have = {e[0]: len(left) + n for n, e in enumerate(rights)}
                rhs = jnp.concatenate(
                    [every(have[w], line) if w in have else jnp.zeros((deep, half), bf16)
                     for w in range(4)], axis=0)
                chi = chi + lax.dot_general(lhs, rhs, (((1,), (1,)), ((), ())),
                                            preferred_element_type=f32)
            for n, e in enumerate(left):
                into = direct_sum if e[0] == S else swapped_sum
                into[e[1] * deep:(e[1] + 1) * deep] += chi[n * deep:(n + 1) * deep]

        each(stop - start, strip)

    mine_x, mine_s, mine_t = (layer.at[array] for array in range(3))

    @pl.when(z == 0)
    def _():
        stretch(0, 5, [(S, 0, mine_s, 0), (S, 1, hub.at[1], 0)],
                [(0, mine_x, 0), (1, hub.at[0], 0)])

    @pl.when(z == 1)
    def _():
        inner = [(S, 1, mine_s, 0), (S, 0, hub.at[1], 5)]
        rights = [(1, mine_x, 0), (0, hub.at[0], 5)]
        stretch(5, 6, inner, rights)
        stretch(6, 8, inner + [(S, 2, hub.at[2], 6), (S, 3, hub.at[3], 6),
                               (T, 2, hub.at[4], 6), (T, 3, hub.at[5], 6)], rights)

    @pl.when(z == 2)
    def _():
        inner = [(S, 2, mine_s, 0), (T, 2, mine_t, 0)]
        rights = [(2, mine_x, 0), (0, hub.at[0], 0), (1, hub.at[1], 0)]
        stretch(0, 3, inner + [(S, 3, hub.at[2], 0), (T, 3, hub.at[3], 0)], rights)
        stretch(3, 6, inner, rights)
        stretch(6, 8, inner[:1], rights[:1])

    @pl.when(z == 3)
    def _():
        inner = [(S, 3, mine_s, 0), (T, 3, mine_t, 0)]
        rights = [(3, mine_x, 0), (2, hub.at[2], 3), (0, hub.at[0], 3), (1, hub.at[1], 3)]
        stretch(0, 3, inner[:1], rights[:1])
        stretch(3, 6, inner, rights)
        stretch(6, 8, inner, rights[:2])

    shape = direct_sum.shape
    down = lax.broadcasted_iota(jnp.int32, shape, 0) // deep
    along = lax.broadcasted_iota(jnp.int32, shape, 1) // deep
    straight = (along <= down) | ((along < 2) & (down < 2))
    turned = (along < down) & (down >= 2)
    value = jnp.where(straight, direct_sum[...], 0.0)
    value = value + jnp.where(turned, swapped_sum[...], 0.0).T
    part[...] = value.reshape(part.shape)

    copies = []
    for k in row_steps:
        to_row = partner(me_row, k, rows)[0]
        copies.append(remote(part.at[to_row], landed.at[k],
                             row_send.at[k], row_recv.at[k], to_row, me_col))
    for copy in copies:
        copy.start()
    value = part[me_row]
    for copy in copies:
        copy.wait()
    for k in range(1, rows):
        value = value + landed[k]
    total[...] = value
    copies = []
    for k in range(1, cols):
        to_col = partner(me_col, k, cols)[0]
        copies.append(remote(total, others.at[me_col],
                             col_send.at[k], col_recv.at[k], me_row, to_col))
    for copy in copies:
        copy.start()
    others[me_col] = value
    for copy in copies:
        copy.wait()
    value = others[0]
    for k in range(1, cols):
        value = value + others[k]
    out_ref[...] = value

    def drain(h):
        @pl.when(y == core)
        def _():
            to_mate(h).wait_send()

        @pl.when(y != core)
        def _():
            over(h, 0).wait_send()
            over(h, 1).wait_send()
        for which in range(3):
            gather_x(h, which).wait_send()
        y_copy(0, h).wait_send()

        @pl.when(z >= 2)
        def _():
            y_copy(1, h).wait_send()
        for k in range(2):
            for w in range(4):
                @pl.when(z == w)
                def _():
                    for i, entry in enumerate(sends[w]):
                        z_copy(i, entry, k, h).wait_send()

            @pl.when(z == 2)
            def _():
                for i, entry in enumerate(passed):
                    pass_copy(i, entry, k, h).wait_send()

    each(chunks, drain)


def layered(rows, cols, three_centre, tensor_pattern, occ_density, virt_density, density_pattern):
    aux, local, orb = three_centre.shape
    share_rows = occ_density.shape[0] // 2
    half, unit, total = orb // 2, local // 8, rows * aux
    bf16, f32 = jnp.bfloat16, jnp.float32
    chunks = aux // 4
    dma = pltpu.SemaphoreType.DMA
    vmem = pl.BlockSpec(memory_space=pltpu.VMEM)
    smem = pl.BlockSpec(memory_space=pltpu.SMEM)
    hbm = pl.BlockSpec(memory_space=pltpu.MemorySpace.HBM)
    return pl.pallas_call(
        functools.partial(layered_kernel, rows, cols, chunks),
        out_shape=jax.ShapeDtypeStruct((aux, total), f32),
        in_specs=[hbm, smem, hbm, hbm, smem],
        out_specs=vmem,
        scratch_shapes=[
            pltpu.VMEM((aux, cols, local, orb), bf16),
            pltpu.VMEM((3, 2, aux, local, half), bf16),
            pltpu.VMEM((2, aux, local, half), bf16),
            pltpu.VMEM((6, 2, aux, 6 * unit, half), bf16),
            pltpu.VMEM((8, half // BS, 2 * aux * unit, BS), f32),
            pltpu.VMEM((total, total), f32),
            pltpu.VMEM((total, total), f32),
            pltpu.VMEM((rows, aux, total), f32),
            pltpu.VMEM((rows, aux, total), f32),
            pltpu.VMEM((aux, total), f32),
            pltpu.VMEM((cols, aux, total), f32),
            pltpu.VMEM((rows, 2, share_rows, orb), bf16),
            pltpu.VMEM((rows, 2, share_rows, orb), bf16),
            pltpu.VMEM((2, orb, half), bf16),
            pltpu.VMEM((2, 2 * local, orb), bf16),
            dma((chunks,)), dma((2 + chunks,)),
            dma((2, rows)), dma((2, rows)), dma((2,)), dma((2,)),
            dma((2, chunks)), dma((2, chunks)), dma((3, chunks)), dma((3, chunks)),
            dma((2, chunks)), dma((2, chunks)), dma((4, 2, chunks)), dma((6, 2, chunks)),
            dma((2, 2, chunks)), dma((rows,)), dma((rows,)), dma((cols,)), dma((cols,)),
        ],
        compiler_params=pltpu.CompilerParams(
            collective_id=1, has_side_effects=True, vmem_limit_bytes=67_000_000),
    )(three_centre, tensor_pattern.transpose(1, 2, 0), occ_density, virt_density,
      density_pattern)


def staged(three_centre, tensor_pattern, occ_density, virt_density, density_pattern):
    aux_count = three_centre.shape[0]
    local_rows = three_centre.shape[1]
    orbital_count = three_centre.shape[2]
    offset = lax.axis_index("col") * local_rows
    row_blocks = (offset + jnp.arange(local_rows, dtype=jnp.int32)) // BS
    pattern_rows = jnp.take(tensor_pattern, row_blocks, axis=1)
    tensor_mask = jnp.repeat(pattern_rows, BS, 2).astype(jnp.bfloat16)
    masked = three_centre * tensor_mask
    occupied_full, virtual_full = (
        lax.all_gather(occ_density, "row", axis=0, tiled=True),
        lax.all_gather(virt_density, "row", axis=0, tiled=True),
    )
    density_mask = expand_blocks(density_pattern, BS, 0, 1).astype(jnp.bfloat16)
    occupied = occupied_full * density_mask
    virtual = virtual_full * density_mask
    moved = jnp.dot(
        masked.reshape(aux_count * local_rows, orbital_count),
        virtual,
        preferred_element_type=jnp.float32,
    ).astype(jnp.bfloat16)
    moved = moved.reshape(aux_count, local_rows, orbital_count)
    moved_cols, regrouped = (
        lax.all_to_all(moved, "col", split_axis=2, concat_axis=1, tiled=True),
        lax.all_to_all(masked, "col", split_axis=2, concat_axis=1, tiled=True),
    )
    second = jnp.einsum(
        "lm,pms->pls", occupied, moved_cols, preferred_element_type=jnp.float32
    ).astype(jnp.bfloat16)
    grouped_left, grouped_right = (
        lax.all_to_all(second, "row", split_axis=1, concat_axis=0, tiled=True),
        lax.all_to_all(regrouped, "row", split_axis=1, concat_axis=0, tiled=True),
    )
    total_aux = grouped_left.shape[0]
    left_flat = grouped_left.reshape(total_aux, -1)
    right_flat = grouped_right.reshape(total_aux, -1)
    partial_chi = lax.dot_general(
        left_flat, right_flat, (((1,), (1,)), ((), ())), preferred_element_type=jnp.float32
    )
    row_summed = lax.psum_scatter(partial_chi, "row", scatter_dimension=0, tiled=True)
    return lax.psum(row_summed, "col")


def solution(mesh):
    rows, cols = mesh.shape["row"], mesh.shape["col"]

    def per_device(three_centre, tensor_pattern, occ_density, virt_density, density_pattern):
        aux, local, orb = three_centre.shape
        aligned = (
            local % (16 * rows) == 0 and occ_density.shape[0] % (16 * cols) == 0
            and orb % (128 * cols) == 0 and BS % local == 0 and aux % 8 == 0
        )
        args = (three_centre, tensor_pattern, occ_density, virt_density, density_pattern)
        if aligned and rows == 8 and cols == 4 and local == BS and orb == cols * local:
            return layered(rows, cols, *args)
        return direct(rows, cols, *args) if aligned else staged(*args)

    in_specs = (P("row", "col", None), P("row", None, None), P("row", None), P("row", None), P())
    out_specs = P("row", None)
    return jax.shard_map(
        per_device, mesh=mesh, in_specs=in_specs, out_specs=out_specs, check_vma=False
    )
```

```python
import functools

import jax
import jax.numpy as jnp
from jax import lax
from jax.experimental import pallas as pl
from jax.experimental.pallas import tpu as pltpu
from jax.sharding import PartitionSpec as P

BS = 128
MESH = pl.DeviceIdType.MESH


def expand_blocks(pattern, block_size, first, second):
    return jnp.repeat(jnp.repeat(pattern, block_size, first), block_size, second)


def partner(me, k, count):
    if count & (count - 1):
        return lax.rem(me + k, count), lax.rem(me + count - k, count)
    bit, other = 1, me
    while bit < count:
        if k & bit:
            other = other + bit - 2 * bit * ((me // bit) % 2)
        bit *= 2
    return other, other


def near_first(count):
    half = [k for k in range(2, count // 2)]
    return half + [1] * (count > 1) + [k for k in range(max(2, count // 2), count)]


def greet(me_row, me_col, rows, cols):
    barrier = pltpu.get_barrier_semaphore()
    for i in range(rows):
        for j in range(cols):
            if i or j:
                pl.semaphore_signal(
                    barrier,
                    inc=1,
                    device_id=(lax.rem(me_row + i, rows), lax.rem(me_col + j, cols)),
                    device_id_type=MESH,
                )
    pl.semaphore_wait(barrier, rows * cols - 1)


def exchange_kernel(
    rows, cols, chunks,
    tensor_ref, pattern_ref, occ_ref, virt_ref, density_ref,
    out_ref,
    b_in, s_in, b_lines, wide_rows, part, landed, total, others,
    masked, virt_all, occ_all, moved, moved_cols, second,
    gather_send, gather_recv, spread_send, spread_recv,
    b_send, b_recv, m_send, m_recv, s_send, s_recv, own_sem, load_sem, row_send, row_recv, col_send, col_recv,
):
    me_row, me_col = lax.axis_index("row"), lax.axis_index("col")
    aux, local, orb = tensor_ref.shape
    strip = local // rows
    wide = orb // cols
    blocks = orb // BS
    quarter = virt_ref.shape[0] // cols
    row_steps = near_first(rows)

    def remote(src, dst, send, recv, to_row, to_col):
        copy = pltpu.make_async_remote_copy(
            src_ref=src, dst_ref=dst, send_sem=send, recv_sem=recv,
            device_id=(to_row, to_col), device_id_type=MESH,
        )
        copy.start()
        return copy

    load = pltpu.make_async_copy(tensor_ref, masked, load_sem)
    load.start()
    greet(me_row, me_col, rows, cols)

    share = pl.ds(pl.multiple_of(me_col * quarter, quarter), quarter)
    gathers = []
    owns = []
    for d, (src, dst) in enumerate(((virt_ref, virt_all), (occ_ref, occ_all))):
        own = pltpu.make_async_copy(src.at[share], dst.at[me_row, me_col], own_sem.at[d])
        own.start()
        owns.append(own)
        gathers.append([
            remote(src.at[share], dst.at[me_row, me_col],
                   gather_send.at[d, k], gather_recv.at[d, k],
                   partner(me_row, k, rows)[0], me_col)
            for k in row_steps
        ])

    block_row = (me_col * local) // BS

    def mask_one(p, carry):
        for j in range(blocks):
            keep = pattern_ref[block_row, j, p].astype(jnp.float32)
            piece = masked[p, :, j * BS:(j + 1) * BS].astype(jnp.float32)
            masked[p, :, j * BS:(j + 1) * BS] = (piece * keep).astype(jnp.bfloat16)
        return carry

    load.wait()
    lax.fori_loop(0, aux, mask_one, 0)

    b_copies = []
    for k in row_steps:
        to_row = partner(me_row, k, rows)[0]
        theirs = pl.ds(pl.multiple_of(to_row * strip, strip), strip)
        b_copies.append(remote(masked.at[:, theirs, :], b_in.at[me_row],
                               b_send.at[k], b_recv.at[k], to_row, me_col))
    own_part = pl.ds(pl.multiple_of(me_row * strip, strip), strip)
    own_b = pltpu.make_async_copy(masked.at[:, own_part, :], b_in.at[me_row], own_sem.at[2])
    own_b.start()

    spreads = []
    for d, full in enumerate((virt_all, occ_all)):
        owns[d].wait()
        for copy in gathers[d]:
            copy.wait_recv()
        spreads.append([
            remote(full.at[:, me_col], full.at[:, me_col],
                   spread_send.at[d, k], spread_recv.at[d, k],
                   me_row, partner(me_col, k, cols)[0])
            for k in range(1, cols)
        ])

    def take_density(full, d):
        for copy in spreads[d]:
            copy.wait()
        for copy in gathers[d]:
            copy.wait_send()
        values = full[...].reshape(orb, orb)
        lines = []
        for i in range(blocks):
            line = []
            for j in range(blocks):
                keep = density_ref[i, j].astype(jnp.float32)
                piece = values[i * BS:(i + 1) * BS, j * BS:(j + 1) * BS].astype(jnp.float32)
                line.append((piece * keep).astype(jnp.bfloat16))
            lines.append(jnp.concatenate(line, axis=1))
        full[...] = jnp.concatenate(lines, axis=0).reshape(full.shape)

    take_density(virt_all, 0)

    def move_one(p, carry):
        product = jnp.dot(masked[p], virt_all[...].reshape(orb, orb),
                          preferred_element_type=jnp.float32).astype(jnp.bfloat16)
        for j in range(cols):
            moved[j, p] = product[:, j * wide:(j + 1) * wide]
        return carry

    span = aux // chunks
    m_copies = []
    for h in range(chunks):
        lax.fori_loop(h * span, (h + 1) * span, move_one, 0)
        piece = pl.ds(h * span, span)
        copies = []
        for k in range(1, cols):
            to_col = partner(me_col, k, cols)[0]
            copies.append(remote(moved.at[to_col, piece], moved_cols.at[me_col, piece],
                                 m_send.at[h, k], m_recv.at[h, k], me_row, to_col))
        own = pltpu.make_async_copy(moved.at[me_col, piece], moved_cols.at[me_col, piece],
                                    own_sem.at[5 + h])
        own.start()
        m_copies.append(copies + [own])

    take_density(occ_all, 1)

    def second_two(p, carry):
        rhs = jnp.concatenate(
            [moved_cols[:, 2 * p + h].reshape(orb, wide) for h in range(2)], axis=1)
        product = jnp.dot(occ_all[...].reshape(orb, orb), rhs,
                          preferred_element_type=jnp.float32).astype(jnp.bfloat16)
        for h in range(2):
            second[2 * p + h] = product[:, h * wide:(h + 1) * wide]
        return carry

    lanes = pl.ds(pl.multiple_of(me_col * wide, wide), wide)

    def strip_of(to_row, to_col):
        return pl.ds(pl.multiple_of(to_col * local + to_row * strip, strip), strip)

    s_copies = [[] for _ in range(chunks)]
    for h in range(chunks):
        piece = pl.ds(h * span, span)
        for copy in m_copies[h]:
            copy.wait()
        lax.fori_loop(h * span // 2, (h + 1) * span // 2, second_two, 0)
        for k in [0] + row_steps:
            for q in range(cols):
                if k or q:
                    to_row, to_col = partner(me_row, k, rows)[0], partner(me_col, q, cols)[0]
                    s_copies[h].append(remote(
                        second.at[piece, strip_of(to_row, to_col), :],
                        s_in.at[me_row, piece, :, lanes],
                        s_send.at[h, k, q], s_recv.at[h, k, q], to_row, to_col))
    own_s = pltpu.make_async_copy(second.at[:, strip_of(me_row, me_col), :],
                                  s_in.at[me_row, :, :, lanes], own_sem.at[4])
    own_s.start()

    def widen(p, carry):
        rows_at = pl.ds(pl.multiple_of(p * aux * strip, aux * strip), aux * strip)
        for j in range(orb // BS):
            wide_rows[j, rows_at, :] = b_in[p, :, :, j * BS:(j + 1) * BS].reshape(
                aux * strip, BS).astype(jnp.float32)
        return carry

    def every(line, count):
        return jnp.concatenate(
            [wide_rows[j, pl.ds(line, count, stride=strip), :] for j in range(orb // BS)],
            axis=1).astype(jnp.bfloat16)

    own_b.wait()
    for copy in b_copies:
        copy.wait()
    lax.fori_loop(0, rows, widen, 0)
    for line in range(strip):
        b_lines[line] = every(line, rows * aux)

    own_s.wait()
    for h in range(chunks):
        for copy in s_copies[h]:
            copy.wait()
        count = rows * span
        for j in range(orb // BS):
            wide_rows[j, 0:count * strip, :] = s_in[
                :, h * span:(h + 1) * span, :, j * BS:(j + 1) * BS].reshape(
                count * strip, BS).astype(jnp.float32)
        chi = jnp.zeros((count, rows * aux), jnp.float32)
        for line in range(strip):
            chi = chi + lax.dot_general(every(line, count), b_lines[line], (((1,), (1,)), ((), ())),
                                        preferred_element_type=jnp.float32)
        part[:, h * span:(h + 1) * span, :] = chi.reshape(rows, span, rows * aux)

    copies = []
    for k in row_steps:
        to_row = partner(me_row, k, rows)[0]
        copies.append(remote(part.at[to_row], landed.at[k],
                             row_send.at[k], row_recv.at[k], to_row, me_col))
    value = part[me_row]
    for copy in copies:
        copy.wait()
    for k in range(1, rows):
        value = value + landed[k]
    total[...] = value
    copies = []
    for k in range(1, cols):
        to_col = partner(me_col, k, cols)[0]
        copies.append(remote(total, others.at[me_col],
                             col_send.at[k], col_recv.at[k], me_row, to_col))
    others[me_col] = value
    for copy in copies:
        copy.wait()
    value = others[0]
    for k in range(1, cols):
        value = value + others[k]
    out_ref[...] = value


def direct(rows, cols, three_centre, tensor_pattern, occ_density, virt_density, density_pattern):
    aux, local, orb = three_centre.shape
    strip, wide = local // rows, orb // cols
    quarter = occ_density.shape[0] // cols
    bf16 = jnp.bfloat16
    chunks = aux // 8
    total = rows * aux
    f32 = jnp.float32
    dma = pltpu.SemaphoreType.DMA
    vmem = pl.BlockSpec(memory_space=pltpu.VMEM)
    smem = pl.BlockSpec(memory_space=pltpu.SMEM)
    hbm = pl.BlockSpec(memory_space=pltpu.MemorySpace.HBM)
    return pl.pallas_call(
        functools.partial(exchange_kernel, rows, cols, chunks),
        out_shape=jax.ShapeDtypeStruct((aux, total), f32),
        in_specs=[hbm, smem, hbm, hbm, smem],
        out_specs=vmem,
        scratch_shapes=[
            pltpu.VMEM((rows, aux, strip, orb), bf16),
            pltpu.VMEM((rows, aux, strip, orb), bf16),
            pltpu.VMEM((strip, total, orb), bf16),
            pltpu.VMEM((orb // BS, total * strip, BS), f32),
            pltpu.VMEM((rows, aux, total), f32),
            pltpu.VMEM((rows, aux, total), f32),
            pltpu.VMEM((aux, total), f32),
            pltpu.VMEM((cols, aux, total), f32),
            pltpu.VMEM((aux, local, orb), bf16),
            pltpu.VMEM((rows, cols, quarter, orb), bf16),
            pltpu.VMEM((rows, cols, quarter, orb), bf16),
            pltpu.VMEM((cols, aux, local, wide), bf16),
            pltpu.VMEM((cols, aux, local, wide), bf16),
            pltpu.VMEM((aux, orb, wide), bf16),
            dma((2, rows)), dma((2, rows)), dma((2, cols)), dma((2, cols)),
            dma((rows,)), dma((rows,)), dma((chunks, cols)), dma((chunks, cols)),
            dma((chunks, rows, cols)), dma((chunks, rows, cols)), dma((5 + chunks,)), dma(()),
            dma((rows,)), dma((rows,)), dma((cols,)), dma((cols,)),
        ],
        compiler_params=pltpu.CompilerParams(
            collective_id=0, has_side_effects=True, vmem_limit_bytes=67_000_000),
    )(three_centre, tensor_pattern.transpose(1, 2, 0), occ_density, virt_density,
      density_pattern)


def layered_kernel(
    rows, cols, chunks,
    tensor_ref, pattern_ref, occ_ref, virt_ref, density_ref,
    out_ref,
    whole, layer, stage, hub, wide_rows, direct_sum, swapped_sum, part, landed, total, others,
    virt_all, occ_all, right, lefts,
    load_sem, own_sem, gather_send, gather_recv, spread_send, spread_recv,
    cut_send, cut_recv, x_send, x_recv, y_send, y_recv, z_send, z_recv,
    pass_send, row_send, row_recv, col_send, col_recv,
):
    me_row, me_col = lax.axis_index("row"), lax.axis_index("col")
    z, y = me_row // 2, me_row % 2
    x, core = me_col // 2, me_col % 2
    aux, local, orb = tensor_ref.shape
    unit = local // 8
    half = orb // 2
    blocks = orb // BS
    span = aux // chunks
    quarter = virt_ref.shape[0] // cols
    row_steps = near_first(rows)
    bf16, f32 = jnp.bfloat16, jnp.float32
    X, S, T = 0, 1, 2
    mate_col, across_col = 2 * x + 1 - core, 2 * (1 - x) + core
    diagonal_col = 2 * (1 - x) + 1 - core
    over_row = 2 * z + 1 - y

    def remote(src, dst, send, recv, to_row, to_col):
        return pltpu.make_async_remote_copy(
            src_ref=src, dst_ref=dst, send_sem=send, recv_sem=recv,
            device_id=(to_row, to_col), device_id_type=MESH,
        )

    def of(h):
        return pl.ds(pl.multiple_of(h * span, span), span)

    def lanes(c):
        return pl.ds(pl.multiple_of(c * half, half), half)

    def load(h):
        return pltpu.make_async_copy(tensor_ref.at[of(h)], whole.at[of(h), me_col], load_sem.at[h])

    def each(count, body):
        def step(i, carry):
            body(i)
            return carry
        lax.fori_loop(0, count, step, 0)

    each(chunks, lambda h: load(h).start())
    barrier = pltpu.get_barrier_semaphore()
    met = [(lax.rem(me_row + i, rows), me_col) for i in range(1, rows)]
    met += [(me_row, lax.rem(me_col + j, cols)) for j in range(1, cols)] + [(over_row, mate_col)]
    for device in met:
        pl.semaphore_signal(barrier, inc=1, device_id=device, device_id_type=MESH)
    pl.semaphore_wait(barrier, len(met))

    share = pl.ds(pl.multiple_of(me_col * quarter, quarter), quarter)
    gathers, owns = [], []
    for d, (src, dst) in enumerate(((virt_ref, virt_all), (occ_ref, occ_all))):
        own = pltpu.make_async_copy(src.at[share], dst.at[me_row, me_col], own_sem.at[d])
        own.start()
        owns.append(own)
        copies = [
            remote(src.at[share], dst.at[me_row, me_col],
                   gather_send.at[d, k], gather_recv.at[d, k],
                   partner(me_row, k, rows)[0], me_col)
            for k in row_steps
        ]
        for copy in copies:
            copy.start()
        gathers.append(copies)

    block_row = (me_col * local) // BS

    def keep(h):
        return pltpu.make_async_copy(
            whole.at[of(h), me_col, :, lanes(core)], layer.at[X, y, of(h)], own_sem.at[2 + h])

    def to_mate(h):
        return remote(whole.at[of(h), me_col, :, lanes(1 - core)], layer.at[X, y, of(h)],
                      cut_send.at[0, h], cut_recv.at[0, h], me_row, mate_col)

    def over(h, c):
        return remote(whole.at[of(h), me_col, :, c * half:(c + 1) * half], layer.at[X, y, of(h)],
                      cut_send.at[c, h], cut_recv.at[1, h], over_row, 2 * x + c)

    def gather_x(h, which):
        block = across_col if which == 2 else me_col
        to_col = across_col if which == 1 else mate_col
        piece = whole.at[of(h), block]
        return remote(piece, piece, x_send.at[which, h], x_recv.at[which, h], me_row, to_col)

    def first(h):
        load(h).wait()

        def mask_one(i):
            p = h * span + i
            for j in range(blocks):
                kept = pattern_ref[block_row, j, p].astype(f32)
                piece = whole[p, me_col, :, j * BS:(j + 1) * BS].astype(f32)
                whole[p, me_col, :, j * BS:(j + 1) * BS] = (piece * kept).astype(bf16)

        each(span, mask_one)

        @pl.when(y == core)
        def _():
            keep(h).start()
            to_mate(h).start()

        @pl.when(y != core)
        def _():
            over(h, 0).start()
            over(h, 1).start()

        gather_x(h, 0).start()

    each(chunks, first)

    def spread(full, d, which):
        block = full.at[:, across_col if which == 2 else me_col]
        return remote(block, block, spread_send.at[d, which], spread_recv.at[d, which],
                      me_row, across_col if which == 1 else mate_col)

    spreads = []
    for d, full in enumerate((virt_all, occ_all)):
        owns[d].wait()
        for copy in gathers[d]:
            copy.wait_recv()
        copies = [spread(full, d, which) for which in range(3)]
        copies[0].start()
        copies[1].start()
        spreads.append(copies)

    each(chunks, lambda h: gather_x(h, 1).start())

    def plan(near, far):
        both = near + far
        rest = 8 - both
        sends = {
            0: [(X, 2, 0, 0, both), (X, 1, 0, 5, 3), (S, 1, 1, 5, 3)],
            1: [(X, 2, 1, 0, both), (X, 0, 0, 0, 5), (S, 0, 1, 0, 5)],
            2: [(X, 3, 2, near, 8 - near), (S, 1, 2, both, rest), (T, 1, 4, both, rest)],
            3: [(S, 2, 2, 0, near), (S, 1, 3, both, rest), (T, 2, 3, 0, near), (T, 1, 5, both, rest)],
        }
        passed = [(0, 3, 0, near, far), (1, 3, 1, near, far)]
        lands = {w: [(e[2], e[4]) for v in sends.values() for e in v if e[1] == w] for w in range(4)}
        lands[3] += [(e[2], e[4]) for e in passed]
        return sends, passed, lands

    plans = [plan(3, 3), plan(2, 3)]
    near_end, far_end = 3 - core, 6 - core

    def on_layer(w, body):
        for c in range(2):
            pl.when((z == w) & (core == c))(functools.partial(body, *plans[c]))

    def slot(k):
        return y if k == 0 else 1 - y

    def z_copy(i, entry, k, h):
        array, to, at, start, count = entry
        return remote(
            layer.at[array, slot(k), of(h), start * unit:(start + count) * unit],
            hub.at[at, slot(k), of(h), 0:count * unit],
            z_send.at[i, k, h], z_recv.at[at, k, h], 2 * to + y, me_col)

    def pass_copy(i, entry, k, h):
        source, to, at, start, count = entry
        return remote(
            hub.at[source, slot(k), of(h), start * unit:(start + count) * unit],
            hub.at[at, slot(k), of(h), 0:count * unit],
            pass_send.at[i, k, h], z_recv.at[at, k, h], 2 * to + y, me_col)

    def landing(at, count, k, h):
        piece = hub.at[at, slot(k), of(h), 0:count * unit]
        return remote(piece, piece, z_send.at[0, k, h], z_recv.at[at, k, h], over_row, me_col)

    def send_z(arrays, k, h):
        for w in range(4):
            def go(sends, passed, lands):
                for i, entry in enumerate(sends[w]):
                    if entry[0] in arrays:
                        z_copy(i, entry, k, h).start()

            if any(e[0] in arrays for e in plans[0][0][w]):
                on_layer(w, go)

    def cut_in(h):
        @pl.when(y == core)
        def _():
            keep(h).wait()

        @pl.when(y != core)
        def _():
            to_mate(h).wait_recv()
        send_z((X,), 0, h)

    each(chunks, cut_in)

    for copies in spreads:
        copies[1].wait_recv()
        copies[2].start()

    def take_density(full, d):
        for copy in spreads[d]:
            copy.wait_send()
        spreads[d][0].wait_recv()
        spreads[d][2].wait_recv()
        for copy in gathers[d]:
            copy.wait_send()
        values = full[...].reshape(orb, orb)
        lines = []
        for i in range(blocks):
            line = []
            for j in range(blocks):
                kept = density_ref[i, j].astype(f32)
                piece = values[i * BS:(i + 1) * BS, j * BS:(j + 1) * BS].astype(f32)
                line.append((piece * kept).astype(bf16))
            lines.append(jnp.concatenate(line, axis=1))
        full[...] = jnp.concatenate(lines, axis=0).reshape(full.shape)

    take_density(virt_all, 0)
    take_density(occ_all, 1)

    for c in range(2):
        @pl.when(core == c)
        def _():
            values = virt_all[...].reshape(orb, orb)
            right[0] = values[:, c * half:(c + 1) * half]
            right[1] = values[c * half:(c + 1) * half, :].astype(f32).T.astype(bf16)

    per = local // (quarter * cols)
    for k in range(2):
        block = 2 * x + slot(k)
        lefts[0, k * local:(k + 1) * local] = occ_all[pl.ds(block * per, per)].reshape(local, orb)
        for b in range(orb // local):
            @pl.when(block == b)
            def _():
                values = occ_all[...].reshape(orb, orb)
                lefts[1, k * local:(k + 1) * local] = (
                    values[:, b * local:(b + 1) * local].astype(f32).T.astype(bf16))

    def y_copy(d, h):
        return remote(stage.at[d, of(h)], layer.at[S + d, y, of(h)],
                      y_send.at[d, h], y_recv.at[d, h], over_row, me_col)

    def transform(d, p):
        moved = jnp.dot(whole[p].reshape(orb, orb), right[d],
                        preferred_element_type=f32).astype(bf16)
        second = jnp.dot(lefts[d], moved, preferred_element_type=f32).astype(bf16)
        layer[S + d, y, p] = second[:local]
        stage[d, p] = second[local:]

    def late(h):
        y_copy(0, h).wait_recv()

        @pl.when(z >= 2)
        def _():
            y_copy(1, h).wait_recv()
        send_z((S, T), 1, h)

    def hand_on(k, h):
        def go(sends, passed, lands):
            for i, entry in enumerate(passed):
                landing(entry[0], entry[3] + entry[4], k, h).wait_recv()
                pass_copy(i, entry, k, h).start()

        on_layer(2, go)

    lag, soon, far_lag = 8, 2, 8

    def main(h):
        gather_x(h, 1).wait_recv()
        gather_x(h, 2).start()
        gather_x(h, 0).wait_recv()
        gather_x(h, 2).wait_recv()

        def one(i):
            p = h * span + i
            transform(0, p)

            @pl.when(z >= 2)
            def _():
                transform(1, p)

        each(span, one)
        y_copy(0, h).start()

        @pl.when(z >= 2)
        def _():
            y_copy(1, h).start()
        send_z((S, T), 0, h)
        over(h, 0).wait_recv()
        send_z((X,), 1, h)

        @pl.when((y == core) & (h >= lag))
        def _():
            late(h - lag)

        @pl.when((y != core) & (h >= soon))
        def _():
            late(h - soon)

        @pl.when(h >= 2)
        def _():
            hand_on(0, h - 2)

        @pl.when(h >= far_lag)
        def _():
            hand_on(1, h - far_lag)

    each(chunks, main)

    each(2, lambda i: hand_on(0, chunks - 2 + i))
    each(far_lag, lambda i: hand_on(1, chunks - far_lag + i))

    @pl.when(y == core)
    def _():
        each(lag, lambda i: late(chunks - lag + i))

    @pl.when(y != core)
    def _():
        each(soon, lambda i: late(chunks - soon + i))

    def settle(w, slots):
        def go(sends, passed, lands):
            def one(h):
                for at, count in lands[w]:
                    if at in slots:
                        for k in range(2):
                            landing(at, count, k, h).wait_recv()
            each(chunks, one)

        on_layer(w, go)

    direct_sum[...] = jnp.zeros_like(direct_sum)
    swapped_sum[...] = jnp.zeros_like(swapped_sum)
    deep = 2 * aux

    def stretch(start, stop, left, rights):
        def strip(i):
            base = (start + i) * unit
            for n, (ref, shift) in enumerate([e[2:] for e in left] + [e[1:] for e in rights]):
                at = pl.ds(pl.multiple_of(base - shift * unit, unit), unit)
                for j in range(half // BS):
                    wide_rows[n, j] = ref[:, :, at, j * BS:(j + 1) * BS].astype(f32).reshape(
                        deep * unit, BS)

            def every(n, line):
                return jnp.concatenate(
                    [wide_rows[n, j, pl.ds(line, deep, stride=unit), :] for j in range(half // BS)],
                    axis=1).astype(bf16)

            chi = jnp.zeros((deep * len(left), 4 * deep), f32)
            for line in range(unit):
                lhs = jnp.concatenate([every(n, line) for n in range(len(left))], axis=0)
                have = {e[0]: len(left) + n for n, e in enumerate(rights)}
                rhs = jnp.concatenate(
                    [every(have[w], line) if w in have else jnp.zeros((deep, half), bf16)
                     for w in range(4)], axis=0)
                chi = chi + lax.dot_general(lhs, rhs, (((1,), (1,)), ((), ())),
                                            preferred_element_type=f32)
            for n, e in enumerate(left):
                into = direct_sum if e[0] == S else swapped_sum
                into[e[1] * deep:(e[1] + 1) * deep] += chi[n * deep:(n + 1) * deep]

        each(stop - start, strip)

    mine_x, mine_s, mine_t = (layer.at[array] for array in range(3))

    @pl.when(z == 0)
    def _():
        settle(0, (0, 1))
        stretch(0, 5, [(S, 0, mine_s, 0), (S, 1, hub.at[1], 0)],
                [(0, mine_x, 0), (1, hub.at[0], 0)])

    @pl.when(z == 1)
    def _():
        rights = [(1, mine_x, 0), (0, hub.at[0], 5)]
        settle(1, (0, 1))
        stretch(5, 8, [(S, 1, mine_s, 0), (S, 0, hub.at[1], 5)], rights)
        settle(1, (2, 3, 4, 5))
        stretch(far_end, 8, [(S, 2, hub.at[2], far_end), (S, 3, hub.at[3], far_end),
                             (T, 2, hub.at[4], far_end), (T, 3, hub.at[5], far_end)], rights)

    @pl.when(z == 2)
    def _():
        rights = [(2, mine_x, 0), (0, hub.at[0], 0), (1, hub.at[1], 0)]
        inner = [(S, 2, mine_s, 0), (T, 2, mine_t, 0)]
        stretch(far_end, 8, inner[:1], rights[:1])
        stretch(0, far_end, inner, rights)
        settle(2, (2, 3))
        stretch(0, near_end, [(S, 3, hub.at[2], 0), (T, 3, hub.at[3], 0)], rights)

    @pl.when(z == 3)
    def _():
        inner = [(S, 3, mine_s, 0), (T, 3, mine_t, 0)]
        near = [(3, mine_x, 0), (2, hub.at[2], near_end)]
        stretch(0, near_end, inner[:1], near[:1])
        settle(3, (2,))
        stretch(near_end, 8, inner, near)
        settle(3, (0, 1))
        stretch(near_end, far_end, inner, [(0, hub.at[0], near_end), (1, hub.at[1], near_end)])

    shape = direct_sum.shape
    down = lax.broadcasted_iota(jnp.int32, shape, 0) // deep
    along = lax.broadcasted_iota(jnp.int32, shape, 1) // deep
    straight = (along <= down) | ((along < 2) & (down < 2))
    turned = (along < down) & (down >= 2)
    value = jnp.where(straight, direct_sum[...], 0.0)
    value = value + jnp.where(turned, swapped_sum[...], 0.0).T
    part[...] = value.reshape(part.shape)

    copies = []
    for k in row_steps:
        to_row = partner(me_row, k, rows)[0]
        copies.append(remote(part.at[to_row], landed.at[k],
                             row_send.at[k], row_recv.at[k], to_row, me_col))
    for copy in copies:
        copy.start()
    value = part[me_row]
    for copy in copies:
        copy.wait()
    for k in range(1, rows):
        value = value + landed[k]
    total[...] = value
    copies = []
    for k in range(1, cols):
        to_col = partner(me_col, k, cols)[0]
        copies.append(remote(total, others.at[me_col],
                             col_send.at[k], col_recv.at[k], me_row, to_col))
    for copy in copies:
        copy.start()
    others[me_col] = value
    for copy in copies:
        copy.wait()
    value = others[0]
    for k in range(1, cols):
        value = value + others[k]
    out_ref[...] = value

    def drain(h):
        @pl.when(y == core)
        def _():
            to_mate(h).wait_send()

        @pl.when(y != core)
        def _():
            over(h, 0).wait_send()
            over(h, 1).wait_send()
        for which in range(3):
            gather_x(h, which).wait_send()
        y_copy(0, h).wait_send()

        @pl.when(z >= 2)
        def _():
            y_copy(1, h).wait_send()
        for w in range(4):
            def go(sends, passed, lands):
                for k in range(2):
                    for i, entry in enumerate(sends[w]):
                        z_copy(i, entry, k, h).wait_send()
                    if w == 2:
                        for i, entry in enumerate(passed):
                            pass_copy(i, entry, k, h).wait_send()

            on_layer(w, go)

    each(chunks, drain)


def layered(rows, cols, three_centre, tensor_pattern, occ_density, virt_density, density_pattern):
    aux, local, orb = three_centre.shape
    quarter = occ_density.shape[0] // cols
    half, unit, total = orb // 2, local // 8, rows * aux
    bf16, f32 = jnp.bfloat16, jnp.float32
    chunks = aux // 2
    dma = pltpu.SemaphoreType.DMA
    vmem = pl.BlockSpec(memory_space=pltpu.VMEM)
    smem = pl.BlockSpec(memory_space=pltpu.SMEM)
    hbm = pl.BlockSpec(memory_space=pltpu.MemorySpace.HBM)
    return pl.pallas_call(
        functools.partial(layered_kernel, rows, cols, chunks),
        out_shape=jax.ShapeDtypeStruct((aux, total), f32),
        in_specs=[hbm, smem, hbm, hbm, smem],
        out_specs=vmem,
        scratch_shapes=[
            pltpu.VMEM((aux, cols, local, orb), bf16),
            pltpu.VMEM((3, 2, aux, local, half), bf16),
            pltpu.VMEM((2, aux, local, half), bf16),
            pltpu.VMEM((6, 2, aux, 6 * unit, half), bf16),
            pltpu.VMEM((8, half // BS, 2 * aux * unit, BS), f32),
            pltpu.VMEM((total, total), f32),
            pltpu.VMEM((total, total), f32),
            pltpu.VMEM((rows, aux, total), f32),
            pltpu.VMEM((rows, aux, total), f32),
            pltpu.VMEM((aux, total), f32),
            pltpu.VMEM((cols, aux, total), f32),
            pltpu.VMEM((rows, cols, quarter, orb), bf16),
            pltpu.VMEM((rows, cols, quarter, orb), bf16),
            pltpu.VMEM((2, orb, half), bf16),
            pltpu.VMEM((2, 2 * local, orb), bf16),
            dma((chunks,)), dma((2 + chunks,)),
            dma((2, rows)), dma((2, rows)), dma((2, 3)), dma((2, 3)),
            dma((2, chunks)), dma((2, chunks)), dma((3, chunks)), dma((3, chunks)),
            dma((2, chunks)), dma((2, chunks)), dma((4, 2, chunks)), dma((6, 2, chunks)),
            dma((2, 2, chunks)), dma((rows,)), dma((rows,)), dma((cols,)), dma((cols,)),
        ],
        compiler_params=pltpu.CompilerParams(
            collective_id=1, has_side_effects=True, vmem_limit_bytes=67_000_000),
    )(three_centre, tensor_pattern.transpose(1, 2, 0), occ_density, virt_density,
      density_pattern)


def staged(three_centre, tensor_pattern, occ_density, virt_density, density_pattern):
    aux_count = three_centre.shape[0]
    local_rows = three_centre.shape[1]
    orbital_count = three_centre.shape[2]
    offset = lax.axis_index("col") * local_rows
    row_blocks = (offset + jnp.arange(local_rows, dtype=jnp.int32)) // BS
    pattern_rows = jnp.take(tensor_pattern, row_blocks, axis=1)
    tensor_mask = jnp.repeat(pattern_rows, BS, 2).astype(jnp.bfloat16)
    masked = three_centre * tensor_mask
    occupied_full, virtual_full = (
        lax.all_gather(occ_density, "row", axis=0, tiled=True),
        lax.all_gather(virt_density, "row", axis=0, tiled=True),
    )
    density_mask = expand_blocks(density_pattern, BS, 0, 1).astype(jnp.bfloat16)
    occupied = occupied_full * density_mask
    virtual = virtual_full * density_mask
    moved = jnp.dot(
        masked.reshape(aux_count * local_rows, orbital_count),
        virtual,
        preferred_element_type=jnp.float32,
    ).astype(jnp.bfloat16)
    moved = moved.reshape(aux_count, local_rows, orbital_count)
    moved_cols, regrouped = (
        lax.all_to_all(moved, "col", split_axis=2, concat_axis=1, tiled=True),
        lax.all_to_all(masked, "col", split_axis=2, concat_axis=1, tiled=True),
    )
    second = jnp.einsum(
        "lm,pms->pls", occupied, moved_cols, preferred_element_type=jnp.float32
    ).astype(jnp.bfloat16)
    grouped_left, grouped_right = (
        lax.all_to_all(second, "row", split_axis=1, concat_axis=0, tiled=True),
        lax.all_to_all(regrouped, "row", split_axis=1, concat_axis=0, tiled=True),
    )
    total_aux = grouped_left.shape[0]
    left_flat = grouped_left.reshape(total_aux, -1)
    right_flat = grouped_right.reshape(total_aux, -1)
    partial_chi = lax.dot_general(
        left_flat, right_flat, (((1,), (1,)), ((), ())), preferred_element_type=jnp.float32
    )
    row_summed = lax.psum_scatter(partial_chi, "row", scatter_dimension=0, tiled=True)
    return lax.psum(row_summed, "col")


def solution(mesh):
    rows, cols = mesh.shape["row"], mesh.shape["col"]

    def per_device(three_centre, tensor_pattern, occ_density, virt_density, density_pattern):
        aux, local, orb = three_centre.shape
        aligned = (
            local % (16 * rows) == 0 and occ_density.shape[0] % (16 * cols) == 0
            and orb % (128 * cols) == 0 and BS % local == 0 and aux % 8 == 0
        )
        args = (three_centre, tensor_pattern, occ_density, virt_density, density_pattern)
        if aligned and rows == 8 and cols == 4 and local == BS and orb == cols * local:
            return layered(rows, cols, *args)
        return direct(rows, cols, *args) if aligned else staged(*args)

    in_specs = (P("row", "col", None), P("row", None, None), P("row", None), P("row", None), P())
    out_specs = P("row", None)
    return jax.shard_map(
        per_device, mesh=mesh, in_specs=in_specs, out_specs=out_specs, check_vma=False
    )
```

```python
import functools

import jax
import jax.numpy as jnp
from jax import lax
from jax.experimental import pallas as pl
from jax.experimental.pallas import tpu as pltpu
from jax.sharding import PartitionSpec as P

BS = 128
MESH = pl.DeviceIdType.MESH


def expand_blocks(pattern, block_size, first, second):
    return jnp.repeat(jnp.repeat(pattern, block_size, first), block_size, second)


def partner(me, k, count):
    if count & (count - 1):
        return lax.rem(me + k, count), lax.rem(me + count - k, count)
    bit, other = 1, me
    while bit < count:
        if k & bit:
            other = other + bit - 2 * bit * ((me // bit) % 2)
        bit *= 2
    return other, other


def near_first(count):
    half = [k for k in range(2, count // 2)]
    return half + [1] * (count > 1) + [k for k in range(max(2, count // 2), count)]


def greet(me_row, me_col, rows, cols):
    barrier = pltpu.get_barrier_semaphore()
    for i in range(rows):
        for j in range(cols):
            if i or j:
                pl.semaphore_signal(
                    barrier,
                    inc=1,
                    device_id=(lax.rem(me_row + i, rows), lax.rem(me_col + j, cols)),
                    device_id_type=MESH,
                )
    pl.semaphore_wait(barrier, rows * cols - 1)


def exchange_kernel(
    rows, cols, chunks,
    tensor_ref, pattern_ref, occ_ref, virt_ref, density_ref,
    out_ref,
    b_in, s_in, b_lines, wide_rows, part, landed, total, others,
    masked, virt_all, occ_all, moved, moved_cols, second,
    gather_send, gather_recv, spread_send, spread_recv,
    b_send, b_recv, m_send, m_recv, s_send, s_recv, own_sem, load_sem, row_send, row_recv, col_send, col_recv,
):
    me_row, me_col = lax.axis_index("row"), lax.axis_index("col")
    aux, local, orb = tensor_ref.shape
    strip = local // rows
    wide = orb // cols
    blocks = orb // BS
    quarter = virt_ref.shape[0] // cols
    row_steps = near_first(rows)

    def remote(src, dst, send, recv, to_row, to_col):
        copy = pltpu.make_async_remote_copy(
            src_ref=src, dst_ref=dst, send_sem=send, recv_sem=recv,
            device_id=(to_row, to_col), device_id_type=MESH,
        )
        copy.start()
        return copy

    load = pltpu.make_async_copy(tensor_ref, masked, load_sem)
    load.start()
    greet(me_row, me_col, rows, cols)

    share = pl.ds(pl.multiple_of(me_col * quarter, quarter), quarter)
    gathers = []
    owns = []
    for d, (src, dst) in enumerate(((virt_ref, virt_all), (occ_ref, occ_all))):
        own = pltpu.make_async_copy(src.at[share], dst.at[me_row, me_col], own_sem.at[d])
        own.start()
        owns.append(own)
        gathers.append([
            remote(src.at[share], dst.at[me_row, me_col],
                   gather_send.at[d, k], gather_recv.at[d, k],
                   partner(me_row, k, rows)[0], me_col)
            for k in row_steps
        ])

    block_row = (me_col * local) // BS

    def mask_one(p, carry):
        for j in range(blocks):
            keep = pattern_ref[block_row, j, p].astype(jnp.float32)
            piece = masked[p, :, j * BS:(j + 1) * BS].astype(jnp.float32)
            masked[p, :, j * BS:(j + 1) * BS] = (piece * keep).astype(jnp.bfloat16)
        return carry

    load.wait()
    lax.fori_loop(0, aux, mask_one, 0)

    b_copies = []
    for k in row_steps:
        to_row = partner(me_row, k, rows)[0]
        theirs = pl.ds(pl.multiple_of(to_row * strip, strip), strip)
        b_copies.append(remote(masked.at[:, theirs, :], b_in.at[me_row],
                               b_send.at[k], b_recv.at[k], to_row, me_col))
    own_part = pl.ds(pl.multiple_of(me_row * strip, strip), strip)
    own_b = pltpu.make_async_copy(masked.at[:, own_part, :], b_in.at[me_row], own_sem.at[2])
    own_b.start()

    spreads = []
    for d, full in enumerate((virt_all, occ_all)):
        owns[d].wait()
        for copy in gathers[d]:
            copy.wait_recv()
        spreads.append([
            remote(full.at[:, me_col], full.at[:, me_col],
                   spread_send.at[d, k], spread_recv.at[d, k],
                   me_row, partner(me_col, k, cols)[0])
            for k in range(1, cols)
        ])

    def take_density(full, d):
        for copy in spreads[d]:
            copy.wait()
        for copy in gathers[d]:
            copy.wait_send()
        values = full[...].reshape(orb, orb)
        lines = []
        for i in range(blocks):
            line = []
            for j in range(blocks):
                keep = density_ref[i, j].astype(jnp.float32)
                piece = values[i * BS:(i + 1) * BS, j * BS:(j + 1) * BS].astype(jnp.float32)
                line.append((piece * keep).astype(jnp.bfloat16))
            lines.append(jnp.concatenate(line, axis=1))
        full[...] = jnp.concatenate(lines, axis=0).reshape(full.shape)

    take_density(virt_all, 0)

    def move_one(p, carry):
        product = jnp.dot(masked[p], virt_all[...].reshape(orb, orb),
                          preferred_element_type=jnp.float32).astype(jnp.bfloat16)
        for j in range(cols):
            moved[j, p] = product[:, j * wide:(j + 1) * wide]
        return carry

    span = aux // chunks
    m_copies = []
    for h in range(chunks):
        lax.fori_loop(h * span, (h + 1) * span, move_one, 0)
        piece = pl.ds(h * span, span)
        copies = []
        for k in range(1, cols):
            to_col = partner(me_col, k, cols)[0]
            copies.append(remote(moved.at[to_col, piece], moved_cols.at[me_col, piece],
                                 m_send.at[h, k], m_recv.at[h, k], me_row, to_col))
        own = pltpu.make_async_copy(moved.at[me_col, piece], moved_cols.at[me_col, piece],
                                    own_sem.at[5 + h])
        own.start()
        m_copies.append(copies + [own])

    take_density(occ_all, 1)

    def second_two(p, carry):
        rhs = jnp.concatenate(
            [moved_cols[:, 2 * p + h].reshape(orb, wide) for h in range(2)], axis=1)
        product = jnp.dot(occ_all[...].reshape(orb, orb), rhs,
                          preferred_element_type=jnp.float32).astype(jnp.bfloat16)
        for h in range(2):
            second[2 * p + h] = product[:, h * wide:(h + 1) * wide]
        return carry

    lanes = pl.ds(pl.multiple_of(me_col * wide, wide), wide)

    def strip_of(to_row, to_col):
        return pl.ds(pl.multiple_of(to_col * local + to_row * strip, strip), strip)

    s_copies = [[] for _ in range(chunks)]
    for h in range(chunks):
        piece = pl.ds(h * span, span)
        for copy in m_copies[h]:
            copy.wait()
        lax.fori_loop(h * span // 2, (h + 1) * span // 2, second_two, 0)
        for k in [0] + row_steps:
            for q in range(cols):
                if k or q:
                    to_row, to_col = partner(me_row, k, rows)[0], partner(me_col, q, cols)[0]
                    s_copies[h].append(remote(
                        second.at[piece, strip_of(to_row, to_col), :],
                        s_in.at[me_row, piece, :, lanes],
                        s_send.at[h, k, q], s_recv.at[h, k, q], to_row, to_col))
    own_s = pltpu.make_async_copy(second.at[:, strip_of(me_row, me_col), :],
                                  s_in.at[me_row, :, :, lanes], own_sem.at[4])
    own_s.start()

    def widen(p, carry):
        rows_at = pl.ds(pl.multiple_of(p * aux * strip, aux * strip), aux * strip)
        for j in range(orb // BS):
            wide_rows[j, rows_at, :] = b_in[p, :, :, j * BS:(j + 1) * BS].reshape(
                aux * strip, BS).astype(jnp.float32)
        return carry

    def every(line, count):
        return jnp.concatenate(
            [wide_rows[j, pl.ds(line, count, stride=strip), :] for j in range(orb // BS)],
            axis=1).astype(jnp.bfloat16)

    own_b.wait()
    for copy in b_copies:
        copy.wait()
    lax.fori_loop(0, rows, widen, 0)
    for line in range(strip):
        b_lines[line] = every(line, rows * aux)

    own_s.wait()
    for h in range(chunks):
        for copy in s_copies[h]:
            copy.wait()
        count = rows * span
        for j in range(orb // BS):
            wide_rows[j, 0:count * strip, :] = s_in[
                :, h * span:(h + 1) * span, :, j * BS:(j + 1) * BS].reshape(
                count * strip, BS).astype(jnp.float32)
        chi = jnp.zeros((count, rows * aux), jnp.float32)
        for line in range(strip):
            chi = chi + lax.dot_general(every(line, count), b_lines[line], (((1,), (1,)), ((), ())),
                                        preferred_element_type=jnp.float32)
        part[:, h * span:(h + 1) * span, :] = chi.reshape(rows, span, rows * aux)

    copies = []
    for k in row_steps:
        to_row = partner(me_row, k, rows)[0]
        copies.append(remote(part.at[to_row], landed.at[k],
                             row_send.at[k], row_recv.at[k], to_row, me_col))
    value = part[me_row]
    for copy in copies:
        copy.wait()
    for k in range(1, rows):
        value = value + landed[k]
    total[...] = value
    copies = []
    for k in range(1, cols):
        to_col = partner(me_col, k, cols)[0]
        copies.append(remote(total, others.at[me_col],
                             col_send.at[k], col_recv.at[k], me_row, to_col))
    others[me_col] = value
    for copy in copies:
        copy.wait()
    value = others[0]
    for k in range(1, cols):
        value = value + others[k]
    out_ref[...] = value


def direct(rows, cols, three_centre, tensor_pattern, occ_density, virt_density, density_pattern):
    aux, local, orb = three_centre.shape
    strip, wide = local // rows, orb // cols
    quarter = occ_density.shape[0] // cols
    bf16 = jnp.bfloat16
    chunks = aux // 8
    total = rows * aux
    f32 = jnp.float32
    dma = pltpu.SemaphoreType.DMA
    vmem = pl.BlockSpec(memory_space=pltpu.VMEM)
    smem = pl.BlockSpec(memory_space=pltpu.SMEM)
    hbm = pl.BlockSpec(memory_space=pltpu.MemorySpace.HBM)
    return pl.pallas_call(
        functools.partial(exchange_kernel, rows, cols, chunks),
        out_shape=jax.ShapeDtypeStruct((aux, total), f32),
        in_specs=[hbm, smem, hbm, hbm, smem],
        out_specs=vmem,
        scratch_shapes=[
            pltpu.VMEM((rows, aux, strip, orb), bf16),
            pltpu.VMEM((rows, aux, strip, orb), bf16),
            pltpu.VMEM((strip, total, orb), bf16),
            pltpu.VMEM((orb // BS, total * strip, BS), f32),
            pltpu.VMEM((rows, aux, total), f32),
            pltpu.VMEM((rows, aux, total), f32),
            pltpu.VMEM((aux, total), f32),
            pltpu.VMEM((cols, aux, total), f32),
            pltpu.VMEM((aux, local, orb), bf16),
            pltpu.VMEM((rows, cols, quarter, orb), bf16),
            pltpu.VMEM((rows, cols, quarter, orb), bf16),
            pltpu.VMEM((cols, aux, local, wide), bf16),
            pltpu.VMEM((cols, aux, local, wide), bf16),
            pltpu.VMEM((aux, orb, wide), bf16),
            dma((2, rows)), dma((2, rows)), dma((2, cols)), dma((2, cols)),
            dma((rows,)), dma((rows,)), dma((chunks, cols)), dma((chunks, cols)),
            dma((chunks, rows, cols)), dma((chunks, rows, cols)), dma((5 + chunks,)), dma(()),
            dma((rows,)), dma((rows,)), dma((cols,)), dma((cols,)),
        ],
        compiler_params=pltpu.CompilerParams(
            collective_id=0, has_side_effects=True, vmem_limit_bytes=67_000_000),
    )(three_centre, tensor_pattern.transpose(1, 2, 0), occ_density, virt_density,
      density_pattern)


def layered_kernel(
    rows, cols, chunks,
    tensor_ref, pattern_ref, occ_ref, virt_ref, density_ref,
    out_ref,
    whole, layer, stage, hub, wide_rows, direct_sum, swapped_sum, part, landed, total, others,
    virt_all, occ_all, right, lefts,
    load_sem, own_sem, gather_send, gather_recv, spread_send, spread_recv,
    cut_send, cut_recv, x_send, x_recv, y_send, y_recv, z_send, z_recv,
    pass_send, row_send, row_recv, col_send, col_recv,
):
    me_row, me_col = lax.axis_index("row"), lax.axis_index("col")
    z, y = me_row // 2, me_row % 2
    x, core = me_col // 2, me_col % 2
    aux, local, orb = tensor_ref.shape
    unit = local // 8
    half = orb // 2
    blocks = orb // BS
    span = aux // chunks
    quarter = virt_ref.shape[0] // cols
    row_steps = near_first(rows)
    bf16, f32 = jnp.bfloat16, jnp.float32
    X, S, T = 0, 1, 2
    mate_col, across_col = 2 * x + 1 - core, 2 * (1 - x) + core
    diagonal_col = 2 * (1 - x) + 1 - core
    over_row = 2 * z + 1 - y

    def remote(src, dst, send, recv, to_row, to_col):
        return pltpu.make_async_remote_copy(
            src_ref=src, dst_ref=dst, send_sem=send, recv_sem=recv,
            device_id=(to_row, to_col), device_id_type=MESH,
        )

    def of(h):
        return pl.ds(pl.multiple_of(h * span, span), span)

    def lanes(c):
        return pl.ds(pl.multiple_of(c * half, half), half)

    def load(h):
        return pltpu.make_async_copy(tensor_ref.at[of(h)], whole.at[of(h), me_col], load_sem.at[h])

    def each(count, body):
        def step(i, carry):
            body(i)
            return carry
        lax.fori_loop(0, count, step, 0)

    each(chunks, lambda h: load(h).start())
    barrier = pltpu.get_barrier_semaphore()
    met = [(lax.rem(me_row + i, rows), me_col) for i in range(1, rows)]
    met += [(me_row, lax.rem(me_col + j, cols)) for j in range(1, cols)] + [(over_row, mate_col)]
    for device in met:
        pl.semaphore_signal(barrier, inc=1, device_id=device, device_id_type=MESH)
    pl.semaphore_wait(barrier, len(met))

    share = pl.ds(pl.multiple_of(me_col * quarter, quarter), quarter)
    gathers, owns = [], []
    for d, (src, dst) in enumerate(((virt_ref, virt_all), (occ_ref, occ_all))):
        own = pltpu.make_async_copy(src.at[share], dst.at[me_row, me_col], own_sem.at[d])
        own.start()
        owns.append(own)
        copies = [
            remote(src.at[share], dst.at[me_row, me_col],
                   gather_send.at[d, k], gather_recv.at[d, k],
                   partner(me_row, k, rows)[0], me_col)
            for k in row_steps
        ]
        for copy in copies:
            copy.start()
        gathers.append(copies)

    block_row = (me_col * local) // BS

    def keep(h):
        return pltpu.make_async_copy(
            whole.at[of(h), me_col, :, lanes(core)], layer.at[X, y, of(h)], own_sem.at[2 + h])

    def to_mate(h):
        return remote(whole.at[of(h), me_col, :, lanes(1 - core)], layer.at[X, y, of(h)],
                      cut_send.at[0, h], cut_recv.at[0, h], me_row, mate_col)

    def over(h, c):
        return remote(whole.at[of(h), me_col, :, c * half:(c + 1) * half], layer.at[X, y, of(h)],
                      cut_send.at[c, h], cut_recv.at[1, h], over_row, 2 * x + c)

    def gather_x(h, which):
        block = across_col if which == 2 else me_col
        to_col = across_col if which == 1 else mate_col
        piece = whole.at[of(h), block]
        return remote(piece, piece, x_send.at[which, h], x_recv.at[which, h], me_row, to_col)

    def first(h):
        load(h).wait()

        def mask_one(i):
            p = h * span + i
            for j in range(blocks):
                kept = pattern_ref[block_row, j, p].astype(f32)
                piece = whole[p, me_col, :, j * BS:(j + 1) * BS].astype(f32)
                whole[p, me_col, :, j * BS:(j + 1) * BS] = (piece * kept).astype(bf16)

        each(span, mask_one)

        @pl.when(y == core)
        def _():
            keep(h).start()
            to_mate(h).start()

        @pl.when(y != core)
        def _():
            over(h, 0).start()
            over(h, 1).start()

        gather_x(h, 0).start()

    each(chunks, first)

    def spread(full, d, which):
        block = full.at[:, across_col if which == 2 else me_col]
        return remote(block, block, spread_send.at[d, which], spread_recv.at[d, which],
                      me_row, across_col if which == 1 else mate_col)

    spreads = []
    for d, full in enumerate((virt_all, occ_all)):
        owns[d].wait()
        for copy in gathers[d]:
            copy.wait_recv()
        copies = [spread(full, d, which) for which in range(3)]
        copies[0].start()
        copies[1].start()
        spreads.append(copies)

    each(chunks, lambda h: gather_x(h, 1).start())

    def plan(near, far):
        both = near + far
        rest = 8 - both
        sends = {
            0: [(X, 2, 0, 0, both), (X, 1, 0, 5, 3), (S, 1, 1, 5, 3)],
            1: [(X, 2, 1, 0, both), (X, 0, 0, 0, 5), (S, 0, 1, 0, 5)],
            2: [(X, 3, 2, near, 8 - near), (S, 1, 2, both, rest), (T, 1, 4, both, rest)],
            3: [(S, 2, 2, 0, near), (S, 1, 3, both, rest), (T, 2, 3, 0, near), (T, 1, 5, both, rest)],
        }
        passed = [(0, 3, 0, near, far), (1, 3, 1, near, far)]
        lands = {w: [(e[2], e[4]) for v in sends.values() for e in v if e[1] == w] for w in range(4)}
        lands[3] += [(e[2], e[4]) for e in passed]
        return sends, passed, lands

    plans = [plan(3, 3), plan(2, 3)]
    near_end, far_end = 3 - core, 6 - core

    def on_layer(w, body):
        for c in range(2):
            pl.when((z == w) & (core == c))(functools.partial(body, *plans[c]))

    def slot(k):
        return y if k == 0 else 1 - y

    def z_copy(i, entry, k, h):
        array, to, at, start, count = entry
        return remote(
            layer.at[array, slot(k), of(h), start * unit:(start + count) * unit],
            hub.at[at, slot(k), of(h), 0:count * unit],
            z_send.at[i, k, h], z_recv.at[at, k, h], 2 * to + y, me_col)

    def pass_copy(i, entry, k, h):
        source, to, at, start, count = entry
        return remote(
            hub.at[source, slot(k), of(h), start * unit:(start + count) * unit],
            hub.at[at, slot(k), of(h), 0:count * unit],
            pass_send.at[i, k, h], z_recv.at[at, k, h], 2 * to + y, me_col)

    def landing(at, count, k, h):
        piece = hub.at[at, slot(k), of(h), 0:count * unit]
        return remote(piece, piece, z_send.at[0, k, h], z_recv.at[at, k, h], over_row, me_col)

    def send_z(arrays, k, h):
        for w in range(4):
            def go(sends, passed, lands):
                for i, entry in enumerate(sends[w]):
                    if entry[0] in arrays:
                        z_copy(i, entry, k, h).start()

            if any(e[0] in arrays for e in plans[0][0][w]):
                on_layer(w, go)

    def cut_in(h):
        @pl.when(y == core)
        def _():
            keep(h).wait()

        @pl.when(y != core)
        def _():
            to_mate(h).wait_recv()
        send_z((X,), 0, h)

    each(chunks, cut_in)

    for copies in spreads:
        copies[1].wait_recv()
        copies[2].start()

    def take_density(full, d):
        for copy in spreads[d]:
            copy.wait_send()
        spreads[d][0].wait_recv()
        spreads[d][2].wait_recv()
        for copy in gathers[d]:
            copy.wait_send()
        values = full[...].reshape(orb, orb)
        lines = []
        for i in range(blocks):
            line = []
            for j in range(blocks):
                kept = density_ref[i, j].astype(f32)
                piece = values[i * BS:(i + 1) * BS, j * BS:(j + 1) * BS].astype(f32)
                line.append((piece * kept).astype(bf16))
            lines.append(jnp.concatenate(line, axis=1))
        full[...] = jnp.concatenate(lines, axis=0).reshape(full.shape)

    take_density(virt_all, 0)
    take_density(occ_all, 1)

    for c in range(2):
        @pl.when(core == c)
        def _():
            values = virt_all[...].reshape(orb, orb)
            right[0] = values[:, c * half:(c + 1) * half]
            right[1] = values[c * half:(c + 1) * half, :].astype(f32).T.astype(bf16)

    per = local // (quarter * cols)
    for k in range(2):
        block = 2 * x + slot(k)
        lefts[0, k * local:(k + 1) * local] = occ_all[pl.ds(block * per, per)].reshape(local, orb)
        for b in range(orb // local):
            @pl.when(block == b)
            def _():
                values = occ_all[...].reshape(orb, orb)
                lefts[1, k * local:(k + 1) * local] = (
                    values[:, b * local:(b + 1) * local].astype(f32).T.astype(bf16))

    def y_copy(d, h):
        return remote(stage.at[d, of(h)], layer.at[S + d, y, of(h)],
                      y_send.at[d, h], y_recv.at[d, h], over_row, me_col)

    def transform(d, p):
        moved = jnp.dot(whole[p].reshape(orb, orb), right[d],
                        preferred_element_type=f32).astype(bf16)
        second = jnp.dot(lefts[d], moved, preferred_element_type=f32).astype(bf16)
        layer[S + d, y, p] = second[:local]
        stage[d, p] = second[local:]

    def late(h):
        y_copy(0, h).wait_recv()

        @pl.when(z >= 2)
        def _():
            y_copy(1, h).wait_recv()
        send_z((S, T), 1, h)

    def hand_on(k, h):
        def go(sends, passed, lands):
            for i, entry in enumerate(passed):
                landing(entry[0], entry[3] + entry[4], k, h).wait_recv()
                pass_copy(i, entry, k, h).start()

        on_layer(2, go)

    lag, soon, far_lag = 7, 2, 8

    def main(h):
        gather_x(h, 1).wait_recv()
        gather_x(h, 2).start()
        gather_x(h, 0).wait_recv()
        gather_x(h, 2).wait_recv()

        def one(i):
            p = h * span + i
            transform(0, p)

            @pl.when(z >= 2)
            def _():
                transform(1, p)

        each(span, one)
        y_copy(0, h).start()

        @pl.when(z >= 2)
        def _():
            y_copy(1, h).start()
        send_z((S, T), 0, h)
        over(h, 0).wait_recv()
        send_z((X,), 1, h)

        @pl.when((y == core) & (h >= lag))
        def _():
            late(h - lag)

        @pl.when((y != core) & (h >= soon))
        def _():
            late(h - soon)

        @pl.when(h >= 2)
        def _():
            hand_on(0, h - 2)

        @pl.when(h >= far_lag)
        def _():
            hand_on(1, h - far_lag)

    each(chunks, main)

    each(2, lambda i: hand_on(0, chunks - 2 + i))
    each(far_lag, lambda i: hand_on(1, chunks - far_lag + i))

    @pl.when(y == core)
    def _():
        each(lag, lambda i: late(chunks - lag + i))

    @pl.when(y != core)
    def _():
        each(soon, lambda i: late(chunks - soon + i))

    def settle(w, slots):
        def go(sends, passed, lands):
            def one(h):
                for at, count in lands[w]:
                    if at in slots:
                        for k in range(2):
                            landing(at, count, k, h).wait_recv()
            each(chunks, one)

        on_layer(w, go)

    direct_sum[...] = jnp.zeros_like(direct_sum)
    swapped_sum[...] = jnp.zeros_like(swapped_sum)
    deep = 2 * aux
    gap = BS - 2 * deep

    def stretch(start, stop, left, rights):
        def strip(i):
            base = (start + i) * unit
            for n, (ref, shift) in enumerate([e[2:] for e in left] + [e[1:] for e in rights]):
                at = pl.ds(pl.multiple_of(base - shift * unit, unit), unit)
                for j in range(half // BS):
                    wide_rows[n, j] = ref[:, :, at, j * BS:(j + 1) * BS].astype(f32).reshape(
                        deep * unit, BS)

            def every(n, line):
                return jnp.concatenate(
                    [wide_rows[n, j, pl.ds(line, deep, stride=unit), :] for j in range(half // BS)],
                    axis=1).astype(bf16)

            chi = jnp.zeros((deep * len(left), 2 * BS), f32)
            for line in range(unit):
                lhs = jnp.concatenate([every(n, line) for n in range(len(left))], axis=0)
                have = {e[0]: len(left) + n for n, e in enumerate(rights)}
                pieces = [every(have[w], line) if w in have else jnp.zeros((deep, half), bf16)
                          for w in range(4)]
                empty = [jnp.zeros((gap, half), bf16)]
                rhs = jnp.concatenate(pieces[:2] + empty + pieces[2:] + empty, axis=0)
                chi = chi + lax.dot_general(lhs, rhs, (((1,), (1,)), ((), ())),
                                            preferred_element_type=f32)
            for n, e in enumerate(left):
                into = direct_sum if e[0] == S else swapped_sum
                at = e[1] * deep + gap * (e[1] // 2)
                into[at:at + deep] += chi[n * deep:(n + 1) * deep]

        each(stop - start, strip)

    mine_x, mine_s, mine_t = (layer.at[array] for array in range(3))

    @pl.when(z == 0)
    def _():
        settle(0, (0, 1))
        stretch(0, 5, [(S, 0, mine_s, 0), (S, 1, hub.at[1], 0)],
                [(0, mine_x, 0), (1, hub.at[0], 0)])

    @pl.when(z == 1)
    def _():
        rights = [(1, mine_x, 0), (0, hub.at[0], 5)]
        settle(1, (0, 1))
        stretch(5, 8, [(S, 1, mine_s, 0), (S, 0, hub.at[1], 5)], rights)
        settle(1, (2, 3, 4, 5))
        stretch(far_end, 8, [(S, 2, hub.at[2], far_end), (S, 3, hub.at[3], far_end),
                             (T, 2, hub.at[4], far_end), (T, 3, hub.at[5], far_end)], rights)

    @pl.when(z == 2)
    def _():
        rights = [(2, mine_x, 0), (0, hub.at[0], 0), (1, hub.at[1], 0)]
        inner = [(S, 2, mine_s, 0), (T, 2, mine_t, 0)]
        stretch(far_end, 8, inner[:1], rights[:1])
        stretch(0, far_end, inner, rights)
        settle(2, (2, 3))
        stretch(0, near_end, [(S, 3, hub.at[2], 0), (T, 3, hub.at[3], 0)], rights)

    @pl.when(z == 3)
    def _():
        inner = [(S, 3, mine_s, 0), (T, 3, mine_t, 0)]
        near = [(3, mine_x, 0), (2, hub.at[2], near_end)]
        stretch(0, near_end, inner[:1], near[:1])
        settle(3, (2,))
        stretch(near_end, 8, inner, near)
        settle(3, (0, 1))
        stretch(near_end, far_end, inner, [(0, hub.at[0], near_end), (1, hub.at[1], near_end)])

    shape = direct_sum.shape
    down, along = (lax.broadcasted_iota(jnp.int32, shape, d) for d in range(2))
    down = jnp.where(down < BS, down // deep, 2 + (down - BS) // deep)
    along = jnp.where(along < BS, along // deep, 2 + (along - BS) // deep)
    straight = (along <= down) | ((along < 2) & (down < 2))
    turned = (along < down) & (down >= 2)
    value = jnp.where(straight, direct_sum[...], 0.0)
    value = value + jnp.where(turned, swapped_sum[...], 0.0).T
    for g in range(rows):
        at = g * aux + gap * (g // (rows // 2))
        part[g] = value[at:at + aux]

    upper = me_row // (rows // 2)

    def columns(c):
        return pl.ds(pl.multiple_of(c * BS, BS), BS)

    copies = []
    for k in row_steps:
        to_row = partner(me_row, k, rows)[0]
        if k < rows // 2:
            source, target = part.at[to_row], landed.at[k]
        else:
            source, target = part.at[to_row, :, columns(upper)], landed.at[k, :, columns(upper)]
        copies.append((k, remote(source, target, row_send.at[k], row_recv.at[k], to_row, me_col)))
    for _, copy in copies:
        copy.start()
    value = part[me_row]
    across = jnp.zeros((aux, BS), f32)
    for k, copy in copies:
        copy.wait()
    for k, _ in copies:
        if k < rows // 2:
            value = value + landed[k]
        else:
            across = across + landed[k, :, columns(1 - upper)]
    value = value + jnp.concatenate(
        [jnp.where(upper == 1, across, 0.0), jnp.where(upper == 0, across, 0.0)], axis=1)
    total[...] = value
    copies = []
    for k in range(1, cols):
        to_col = partner(me_col, k, cols)[0]
        copies.append(remote(total, others.at[me_col],
                             col_send.at[k], col_recv.at[k], me_row, to_col))
    for copy in copies:
        copy.start()
    others[me_col] = value
    for copy in copies:
        copy.wait()
    value = others[0]
    for k in range(1, cols):
        value = value + others[k]
    out_ref[:, 0:2 * deep] = value[:, 0:2 * deep]
    out_ref[:, 2 * deep:4 * deep] = value[:, BS:BS + 2 * deep]

    def drain(h):
        @pl.when(y == core)
        def _():
            to_mate(h).wait_send()

        @pl.when(y != core)
        def _():
            over(h, 0).wait_send()
            over(h, 1).wait_send()
        for which in range(3):
            gather_x(h, which).wait_send()
        y_copy(0, h).wait_send()

        @pl.when(z >= 2)
        def _():
            y_copy(1, h).wait_send()
        for w in range(4):
            def go(sends, passed, lands):
                for k in range(2):
                    for i, entry in enumerate(sends[w]):
                        z_copy(i, entry, k, h).wait_send()
                    if w == 2:
                        for i, entry in enumerate(passed):
                            pass_copy(i, entry, k, h).wait_send()

            on_layer(w, go)

    each(chunks, drain)


def layered(rows, cols, three_centre, tensor_pattern, occ_density, virt_density, density_pattern):
    aux, local, orb = three_centre.shape
    quarter = occ_density.shape[0] // cols
    half, unit, total = orb // 2, local // 8, rows * aux
    bf16, f32 = jnp.bfloat16, jnp.float32
    chunks = aux // 2
    dma = pltpu.SemaphoreType.DMA
    vmem = pl.BlockSpec(memory_space=pltpu.VMEM)
    smem = pl.BlockSpec(memory_space=pltpu.SMEM)
    hbm = pl.BlockSpec(memory_space=pltpu.MemorySpace.HBM)
    return pl.pallas_call(
        functools.partial(layered_kernel, rows, cols, chunks),
        out_shape=jax.ShapeDtypeStruct((aux, total), f32),
        in_specs=[hbm, smem, hbm, hbm, smem],
        out_specs=vmem,
        scratch_shapes=[
            pltpu.VMEM((aux, cols, local, orb), bf16),
            pltpu.VMEM((3, 2, aux, local, half), bf16),
            pltpu.VMEM((2, aux, local, half), bf16),
            pltpu.VMEM((6, 2, aux, 6 * unit, half), bf16),
            pltpu.VMEM((8, half // BS, 2 * aux * unit, BS), f32),
            pltpu.VMEM((2 * BS, 2 * BS), f32),
            pltpu.VMEM((2 * BS, 2 * BS), f32),
            pltpu.VMEM((rows, aux, 2 * BS), f32),
            pltpu.VMEM((rows, aux, 2 * BS), f32),
            pltpu.VMEM((aux, 2 * BS), f32),
            pltpu.VMEM((cols, aux, 2 * BS), f32),
            pltpu.VMEM((rows, cols, quarter, orb), bf16),
            pltpu.VMEM((rows, cols, quarter, orb), bf16),
            pltpu.VMEM((2, orb, half), bf16),
            pltpu.VMEM((2, 2 * local, orb), bf16),
            dma((chunks,)), dma((2 + chunks,)),
            dma((2, rows)), dma((2, rows)), dma((2, 3)), dma((2, 3)),
            dma((2, chunks)), dma((2, chunks)), dma((3, chunks)), dma((3, chunks)),
            dma((2, chunks)), dma((2, chunks)), dma((4, 2, chunks)), dma((6, 2, chunks)),
            dma((2, 2, chunks)), dma((rows,)), dma((rows,)), dma((cols,)), dma((cols,)),
        ],
        compiler_params=pltpu.CompilerParams(
            collective_id=1, has_side_effects=True, vmem_limit_bytes=67_000_000),
    )(three_centre, tensor_pattern.transpose(1, 2, 0), occ_density, virt_density,
      density_pattern)


def staged(three_centre, tensor_pattern, occ_density, virt_density, density_pattern):
    aux_count = three_centre.shape[0]
    local_rows = three_centre.shape[1]
    orbital_count = three_centre.shape[2]
    offset = lax.axis_index("col") * local_rows
    row_blocks = (offset + jnp.arange(local_rows, dtype=jnp.int32)) // BS
    pattern_rows = jnp.take(tensor_pattern, row_blocks, axis=1)
    tensor_mask = jnp.repeat(pattern_rows, BS, 2).astype(jnp.bfloat16)
    masked = three_centre * tensor_mask
    occupied_full, virtual_full = (
        lax.all_gather(occ_density, "row", axis=0, tiled=True),
        lax.all_gather(virt_density, "row", axis=0, tiled=True),
    )
    density_mask = expand_blocks(density_pattern, BS, 0, 1).astype(jnp.bfloat16)
    occupied = occupied_full * density_mask
    virtual = virtual_full * density_mask
    moved = jnp.dot(
        masked.reshape(aux_count * local_rows, orbital_count),
        virtual,
        preferred_element_type=jnp.float32,
    ).astype(jnp.bfloat16)
    moved = moved.reshape(aux_count, local_rows, orbital_count)
    moved_cols, regrouped = (
        lax.all_to_all(moved, "col", split_axis=2, concat_axis=1, tiled=True),
        lax.all_to_all(masked, "col", split_axis=2, concat_axis=1, tiled=True),
    )
    second = jnp.einsum(
        "lm,pms->pls", occupied, moved_cols, preferred_element_type=jnp.float32
    ).astype(jnp.bfloat16)
    grouped_left, grouped_right = (
        lax.all_to_all(second, "row", split_axis=1, concat_axis=0, tiled=True),
        lax.all_to_all(regrouped, "row", split_axis=1, concat_axis=0, tiled=True),
    )
    total_aux = grouped_left.shape[0]
    left_flat = grouped_left.reshape(total_aux, -1)
    right_flat = grouped_right.reshape(total_aux, -1)
    partial_chi = lax.dot_general(
        left_flat, right_flat, (((1,), (1,)), ((), ())), preferred_element_type=jnp.float32
    )
    row_summed = lax.psum_scatter(partial_chi, "row", scatter_dimension=0, tiled=True)
    return lax.psum(row_summed, "col")


def solution(mesh):
    rows, cols = mesh.shape["row"], mesh.shape["col"]

    def per_device(three_centre, tensor_pattern, occ_density, virt_density, density_pattern):
        aux, local, orb = three_centre.shape
        aligned = (
            local % (16 * rows) == 0 and occ_density.shape[0] % (16 * cols) == 0
            and orb % (128 * cols) == 0 and BS % local == 0 and aux % 8 == 0
        )
        args = (three_centre, tensor_pattern, occ_density, virt_density, density_pattern)
        if (aligned and rows == 8 and cols == 4 and local == BS and orb == cols * local
                and 4 * aux <= BS):
            return layered(rows, cols, *args)
        return direct(rows, cols, *args) if aligned else staged(*args)

    in_specs = (P("row", "col", None), P("row", None, None), P("row", None), P("row", None), P())
    out_specs = P("row", None)
    return jax.shard_map(
        per_device, mesh=mesh, in_specs=in_specs, out_specs=out_specs, check_vma=False
    )
```

```python
import functools

import jax
import jax.numpy as jnp
from jax import lax
from jax.experimental import pallas as pl
from jax.experimental.pallas import tpu as pltpu
from jax.sharding import PartitionSpec as P

BS = 128
MESH = pl.DeviceIdType.MESH


def expand_blocks(pattern, block_size, first, second):
    return jnp.repeat(jnp.repeat(pattern, block_size, first), block_size, second)


def partner(me, k, count):
    if count & (count - 1):
        return lax.rem(me + k, count), lax.rem(me + count - k, count)
    bit, other = 1, me
    while bit < count:
        if k & bit:
            other = other + bit - 2 * bit * ((me // bit) % 2)
        bit *= 2
    return other, other


def near_first(count):
    half = [k for k in range(2, count // 2)]
    return half + [1] * (count > 1) + [k for k in range(max(2, count // 2), count)]


def greet(me_row, me_col, rows, cols):
    barrier = pltpu.get_barrier_semaphore()
    for i in range(rows):
        for j in range(cols):
            if i or j:
                pl.semaphore_signal(
                    barrier,
                    inc=1,
                    device_id=(lax.rem(me_row + i, rows), lax.rem(me_col + j, cols)),
                    device_id_type=MESH,
                )
    pl.semaphore_wait(barrier, rows * cols - 1)


def exchange_kernel(
    rows, cols, chunks,
    tensor_ref, pattern_ref, occ_ref, virt_ref, density_ref,
    out_ref,
    b_in, s_in, b_lines, wide_rows, part, landed, total, others,
    masked, virt_all, occ_all, moved, moved_cols, second,
    gather_send, gather_recv, spread_send, spread_recv,
    b_send, b_recv, m_send, m_recv, s_send, s_recv, own_sem, load_sem, row_send, row_recv, col_send, col_recv,
):
    me_row, me_col = lax.axis_index("row"), lax.axis_index("col")
    aux, local, orb = tensor_ref.shape
    strip = local // rows
    wide = orb // cols
    blocks = orb // BS
    quarter = virt_ref.shape[0] // cols
    row_steps = near_first(rows)

    def remote(src, dst, send, recv, to_row, to_col):
        copy = pltpu.make_async_remote_copy(
            src_ref=src, dst_ref=dst, send_sem=send, recv_sem=recv,
            device_id=(to_row, to_col), device_id_type=MESH,
        )
        copy.start()
        return copy

    load = pltpu.make_async_copy(tensor_ref, masked, load_sem)
    load.start()
    greet(me_row, me_col, rows, cols)

    share = pl.ds(pl.multiple_of(me_col * quarter, quarter), quarter)
    gathers = []
    owns = []
    for d, (src, dst) in enumerate(((virt_ref, virt_all), (occ_ref, occ_all))):
        own = pltpu.make_async_copy(src.at[share], dst.at[me_row, me_col], own_sem.at[d])
        own.start()
        owns.append(own)
        gathers.append([
            remote(src.at[share], dst.at[me_row, me_col],
                   gather_send.at[d, k], gather_recv.at[d, k],
                   partner(me_row, k, rows)[0], me_col)
            for k in row_steps
        ])

    block_row = (me_col * local) // BS

    def mask_one(p, carry):
        for j in range(blocks):
            keep = pattern_ref[block_row, j, p].astype(jnp.float32)
            piece = masked[p, :, j * BS:(j + 1) * BS].astype(jnp.float32)
            masked[p, :, j * BS:(j + 1) * BS] = (piece * keep).astype(jnp.bfloat16)
        return carry

    load.wait()
    lax.fori_loop(0, aux, mask_one, 0)

    b_copies = []
    for k in row_steps:
        to_row = partner(me_row, k, rows)[0]
        theirs = pl.ds(pl.multiple_of(to_row * strip, strip), strip)
        b_copies.append(remote(masked.at[:, theirs, :], b_in.at[me_row],
                               b_send.at[k], b_recv.at[k], to_row, me_col))
    own_part = pl.ds(pl.multiple_of(me_row * strip, strip), strip)
    own_b = pltpu.make_async_copy(masked.at[:, own_part, :], b_in.at[me_row], own_sem.at[2])
    own_b.start()

    spreads = []
    for d, full in enumerate((virt_all, occ_all)):
        owns[d].wait()
        for copy in gathers[d]:
            copy.wait_recv()
        spreads.append([
            remote(full.at[:, me_col], full.at[:, me_col],
                   spread_send.at[d, k], spread_recv.at[d, k],
                   me_row, partner(me_col, k, cols)[0])
            for k in range(1, cols)
        ])

    def take_density(full, d):
        for copy in spreads[d]:
            copy.wait()
        for copy in gathers[d]:
            copy.wait_send()
        values = full[...].reshape(orb, orb)
        lines = []
        for i in range(blocks):
            line = []
            for j in range(blocks):
                keep = density_ref[i, j].astype(jnp.float32)
                piece = values[i * BS:(i + 1) * BS, j * BS:(j + 1) * BS].astype(jnp.float32)
                line.append((piece * keep).astype(jnp.bfloat16))
            lines.append(jnp.concatenate(line, axis=1))
        full[...] = jnp.concatenate(lines, axis=0).reshape(full.shape)

    take_density(virt_all, 0)

    def move_one(p, carry):
        product = jnp.dot(masked[p], virt_all[...].reshape(orb, orb),
                          preferred_element_type=jnp.float32).astype(jnp.bfloat16)
        for j in range(cols):
            moved[j, p] = product[:, j * wide:(j + 1) * wide]
        return carry

    span = aux // chunks
    m_copies = []
    for h in range(chunks):
        lax.fori_loop(h * span, (h + 1) * span, move_one, 0)
        piece = pl.ds(h * span, span)
        copies = []
        for k in range(1, cols):
            to_col = partner(me_col, k, cols)[0]
            copies.append(remote(moved.at[to_col, piece], moved_cols.at[me_col, piece],
                                 m_send.at[h, k], m_recv.at[h, k], me_row, to_col))
        own = pltpu.make_async_copy(moved.at[me_col, piece], moved_cols.at[me_col, piece],
                                    own_sem.at[5 + h])
        own.start()
        m_copies.append(copies + [own])

    take_density(occ_all, 1)

    def second_two(p, carry):
        rhs = jnp.concatenate(
            [moved_cols[:, 2 * p + h].reshape(orb, wide) for h in range(2)], axis=1)
        product = jnp.dot(occ_all[...].reshape(orb, orb), rhs,
                          preferred_element_type=jnp.float32).astype(jnp.bfloat16)
        for h in range(2):
            second[2 * p + h] = product[:, h * wide:(h + 1) * wide]
        return carry

    lanes = pl.ds(pl.multiple_of(me_col * wide, wide), wide)

    def strip_of(to_row, to_col):
        return pl.ds(pl.multiple_of(to_col * local + to_row * strip, strip), strip)

    s_copies = [[] for _ in range(chunks)]
    for h in range(chunks):
        piece = pl.ds(h * span, span)
        for copy in m_copies[h]:
            copy.wait()
        lax.fori_loop(h * span // 2, (h + 1) * span // 2, second_two, 0)
        for k in [0] + row_steps:
            for q in range(cols):
                if k or q:
                    to_row, to_col = partner(me_row, k, rows)[0], partner(me_col, q, cols)[0]
                    s_copies[h].append(remote(
                        second.at[piece, strip_of(to_row, to_col), :],
                        s_in.at[me_row, piece, :, lanes],
                        s_send.at[h, k, q], s_recv.at[h, k, q], to_row, to_col))
    own_s = pltpu.make_async_copy(second.at[:, strip_of(me_row, me_col), :],
                                  s_in.at[me_row, :, :, lanes], own_sem.at[4])
    own_s.start()

    def widen(p, carry):
        rows_at = pl.ds(pl.multiple_of(p * aux * strip, aux * strip), aux * strip)
        for j in range(orb // BS):
            wide_rows[j, rows_at, :] = b_in[p, :, :, j * BS:(j + 1) * BS].reshape(
                aux * strip, BS).astype(jnp.float32)
        return carry

    def every(line, count):
        return jnp.concatenate(
            [wide_rows[j, pl.ds(line, count, stride=strip), :] for j in range(orb // BS)],
            axis=1).astype(jnp.bfloat16)

    own_b.wait()
    for copy in b_copies:
        copy.wait()
    lax.fori_loop(0, rows, widen, 0)
    for line in range(strip):
        b_lines[line] = every(line, rows * aux)

    own_s.wait()
    for h in range(chunks):
        for copy in s_copies[h]:
            copy.wait()
        count = rows * span
        for j in range(orb // BS):
            wide_rows[j, 0:count * strip, :] = s_in[
                :, h * span:(h + 1) * span, :, j * BS:(j + 1) * BS].reshape(
                count * strip, BS).astype(jnp.float32)
        chi = jnp.zeros((count, rows * aux), jnp.float32)
        for line in range(strip):
            chi = chi + lax.dot_general(every(line, count), b_lines[line], (((1,), (1,)), ((), ())),
                                        preferred_element_type=jnp.float32)
        part[:, h * span:(h + 1) * span, :] = chi.reshape(rows, span, rows * aux)

    copies = []
    for k in row_steps:
        to_row = partner(me_row, k, rows)[0]
        copies.append(remote(part.at[to_row], landed.at[k],
                             row_send.at[k], row_recv.at[k], to_row, me_col))
    value = part[me_row]
    for copy in copies:
        copy.wait()
    for k in range(1, rows):
        value = value + landed[k]
    total[...] = value
    copies = []
    for k in range(1, cols):
        to_col = partner(me_col, k, cols)[0]
        copies.append(remote(total, others.at[me_col],
                             col_send.at[k], col_recv.at[k], me_row, to_col))
    others[me_col] = value
    for copy in copies:
        copy.wait()
    value = others[0]
    for k in range(1, cols):
        value = value + others[k]
    out_ref[...] = value


def direct(rows, cols, three_centre, tensor_pattern, occ_density, virt_density, density_pattern):
    aux, local, orb = three_centre.shape
    strip, wide = local // rows, orb // cols
    quarter = occ_density.shape[0] // cols
    bf16 = jnp.bfloat16
    chunks = aux // 8
    total = rows * aux
    f32 = jnp.float32
    dma = pltpu.SemaphoreType.DMA
    vmem = pl.BlockSpec(memory_space=pltpu.VMEM)
    smem = pl.BlockSpec(memory_space=pltpu.SMEM)
    hbm = pl.BlockSpec(memory_space=pltpu.MemorySpace.HBM)
    return pl.pallas_call(
        functools.partial(exchange_kernel, rows, cols, chunks),
        out_shape=jax.ShapeDtypeStruct((aux, total), f32),
        in_specs=[hbm, smem, hbm, hbm, smem],
        out_specs=vmem,
        scratch_shapes=[
            pltpu.VMEM((rows, aux, strip, orb), bf16),
            pltpu.VMEM((rows, aux, strip, orb), bf16),
            pltpu.VMEM((strip, total, orb), bf16),
            pltpu.VMEM((orb // BS, total * strip, BS), f32),
            pltpu.VMEM((rows, aux, total), f32),
            pltpu.VMEM((rows, aux, total), f32),
            pltpu.VMEM((aux, total), f32),
            pltpu.VMEM((cols, aux, total), f32),
            pltpu.VMEM((aux, local, orb), bf16),
            pltpu.VMEM((rows, cols, quarter, orb), bf16),
            pltpu.VMEM((rows, cols, quarter, orb), bf16),
            pltpu.VMEM((cols, aux, local, wide), bf16),
            pltpu.VMEM((cols, aux, local, wide), bf16),
            pltpu.VMEM((aux, orb, wide), bf16),
            dma((2, rows)), dma((2, rows)), dma((2, cols)), dma((2, cols)),
            dma((rows,)), dma((rows,)), dma((chunks, cols)), dma((chunks, cols)),
            dma((chunks, rows, cols)), dma((chunks, rows, cols)), dma((5 + chunks,)), dma(()),
            dma((rows,)), dma((rows,)), dma((cols,)), dma((cols,)),
        ],
        compiler_params=pltpu.CompilerParams(
            collective_id=0, has_side_effects=True, vmem_limit_bytes=67_000_000),
    )(three_centre, tensor_pattern.transpose(1, 2, 0), occ_density, virt_density,
      density_pattern)


def layered_kernel(
    rows, cols, chunks,
    tensor_ref, pattern_ref, occ_ref, virt_ref, density_ref,
    out_ref,
    whole, layer, stage, hub, wide_rows, direct_sum, swapped_sum, part, landed, total, others,
    virt_all, occ_all, right, lefts,
    load_sem, own_sem, gather_send, gather_recv, spread_send, spread_recv,
    cut_send, cut_recv, x_send, x_recv, y_send, y_recv, z_send, z_recv,
    pass_send, row_send, row_recv, col_send, col_recv,
):
    me_row, me_col = lax.axis_index("row"), lax.axis_index("col")
    z, y = me_row // 2, me_row % 2
    x, core = me_col // 2, me_col % 2
    aux, local, orb = tensor_ref.shape
    unit = local // 8
    half = orb // 2
    blocks = orb // BS
    span = aux // chunks
    quarter = virt_ref.shape[0] // cols
    row_steps = near_first(rows)
    bf16, f32 = jnp.bfloat16, jnp.float32
    X, S, T = 0, 1, 2
    mate_col, across_col = 2 * x + 1 - core, 2 * (1 - x) + core
    diagonal_col = 2 * (1 - x) + 1 - core
    over_row = 2 * z + 1 - y

    def remote(src, dst, send, recv, to_row, to_col):
        return pltpu.make_async_remote_copy(
            src_ref=src, dst_ref=dst, send_sem=send, recv_sem=recv,
            device_id=(to_row, to_col), device_id_type=MESH,
        )

    def of(h):
        return pl.ds(pl.multiple_of(h * span, span), span)

    def lanes(c):
        return pl.ds(pl.multiple_of(c * half, half), half)

    def load(h):
        return pltpu.make_async_copy(tensor_ref.at[of(h)], whole.at[of(h), me_col], load_sem.at[h])

    def each(count, body):
        def step(i, carry):
            body(i)
            return carry
        lax.fori_loop(0, count, step, 0)

    each(chunks, lambda h: load(h).start())
    barrier = pltpu.get_barrier_semaphore()
    met = [(lax.rem(me_row + i, rows), me_col) for i in range(1, rows)]
    met += [(me_row, lax.rem(me_col + j, cols)) for j in range(1, cols)] + [(over_row, mate_col)]
    for device in met:
        pl.semaphore_signal(barrier, inc=1, device_id=device, device_id_type=MESH)
    pl.semaphore_wait(barrier, len(met))

    share = pl.ds(pl.multiple_of(me_col * quarter, quarter), quarter)
    gathers, owns = [], []
    for d, (src, dst) in enumerate(((virt_ref, virt_all), (occ_ref, occ_all))):
        own = pltpu.make_async_copy(src.at[share], dst.at[me_row, me_col], own_sem.at[d])
        own.start()
        owns.append(own)
        copies = [
            remote(src.at[share], dst.at[me_row, me_col],
                   gather_send.at[d, k], gather_recv.at[d, k],
                   partner(me_row, k, rows)[0], me_col)
            for k in row_steps
        ]
        for copy in copies:
            copy.start()
        gathers.append(copies)

    block_row = (me_col * local) // BS

    def keep(h):
        return pltpu.make_async_copy(
            whole.at[of(h), me_col, :, lanes(core)], layer.at[X, y, of(h)], own_sem.at[2 + h])

    def to_mate(h):
        return remote(whole.at[of(h), me_col, :, lanes(1 - core)], layer.at[X, y, of(h)],
                      cut_send.at[0, h], cut_recv.at[0, h], me_row, mate_col)

    def over(h, c):
        return remote(whole.at[of(h), me_col, :, c * half:(c + 1) * half], layer.at[X, y, of(h)],
                      cut_send.at[c, h], cut_recv.at[1, h], over_row, 2 * x + c)

    def gather_x(h, which):
        block = across_col if which == 2 else me_col
        to_col = across_col if which == 1 else mate_col
        piece = whole.at[of(h), block]
        return remote(piece, piece, x_send.at[which, h], x_recv.at[which, h], me_row, to_col)

    def first(h):
        load(h).wait()

        def mask_one(i):
            p = h * span + i
            for j in range(blocks):
                kept = pattern_ref[block_row, j, p].astype(f32)
                piece = whole[p, me_col, :, j * BS:(j + 1) * BS].astype(f32)
                whole[p, me_col, :, j * BS:(j + 1) * BS] = (piece * kept).astype(bf16)

        each(span, mask_one)

        @pl.when(y == core)
        def _():
            keep(h).start()
            to_mate(h).start()

        @pl.when(y != core)
        def _():
            over(h, 0).start()
            over(h, 1).start()

        gather_x(h, 0).start()

    each(chunks, first)

    def spread(full, d, which):
        block = full.at[:, across_col if which == 2 else me_col]
        return remote(block, block, spread_send.at[d, which], spread_recv.at[d, which],
                      me_row, across_col if which == 1 else mate_col)

    spreads = []
    for d, full in enumerate((virt_all, occ_all)):
        owns[d].wait()
        for copy in gathers[d]:
            copy.wait_recv()
        copies = [spread(full, d, which) for which in range(3)]
        copies[0].start()
        copies[1].start()
        spreads.append(copies)

    each(chunks, lambda h: gather_x(h, 1).start())

    def plan(near, far):
        both = near + far
        rest = 8 - both
        sends = {
            0: [(X, 2, 0, 0, both), (X, 1, 0, 5, 3), (S, 1, 1, 5, 3)],
            1: [(X, 2, 1, 0, both), (X, 0, 0, 0, 5), (S, 0, 1, 0, 5)],
            2: [(X, 3, 2, near, 8 - near), (S, 1, 2, both, rest), (T, 1, 4, both, rest)],
            3: [(S, 2, 2, 0, near), (S, 1, 3, both, rest), (T, 2, 3, 0, near), (T, 1, 5, both, rest)],
        }
        passed = [(0, 3, 0, near, far), (1, 3, 1, near, far)]
        lands = {w: [(e[2], e[4]) for v in sends.values() for e in v if e[1] == w] for w in range(4)}
        lands[3] += [(e[2], e[4]) for e in passed]
        return sends, passed, lands

    plans = [plan(3, 3), plan(2, 3)]
    near_end, far_end = 3 - core, 6 - core

    def on_layer(w, body):
        for c in range(2):
            pl.when((z == w) & (core == c))(functools.partial(body, *plans[c]))

    def slot(k):
        return y if k == 0 else 1 - y

    def z_copy(i, entry, k, h):
        array, to, at, start, count = entry
        return remote(
            layer.at[array, slot(k), of(h), start * unit:(start + count) * unit],
            hub.at[at, slot(k), of(h), 0:count * unit],
            z_send.at[i, k, h], z_recv.at[at, k, h], 2 * to + y, me_col)

    def pass_copy(i, entry, k, h):
        source, to, at, start, count = entry
        return remote(
            hub.at[source, slot(k), of(h), start * unit:(start + count) * unit],
            hub.at[at, slot(k), of(h), 0:count * unit],
            pass_send.at[i, k, h], z_recv.at[at, k, h], 2 * to + y, me_col)

    def landing(at, count, k, h):
        piece = hub.at[at, slot(k), of(h), 0:count * unit]
        return remote(piece, piece, z_send.at[0, k, h], z_recv.at[at, k, h], over_row, me_col)

    def send_z(arrays, k, h):
        for w in range(4):
            def go(sends, passed, lands):
                for i, entry in enumerate(sends[w]):
                    if entry[0] in arrays:
                        z_copy(i, entry, k, h).start()

            if any(e[0] in arrays for e in plans[0][0][w]):
                on_layer(w, go)

    def cut_in(h):
        @pl.when(y == core)
        def _():
            keep(h).wait()

        @pl.when(y != core)
        def _():
            to_mate(h).wait_recv()
        send_z((X,), 0, h)

    each(chunks, cut_in)

    for copies in spreads:
        copies[1].wait_recv()
        copies[2].start()

    def take_density(full, d):
        for copy in spreads[d]:
            copy.wait_send()
        spreads[d][0].wait_recv()
        spreads[d][2].wait_recv()
        for copy in gathers[d]:
            copy.wait_send()
        values = full[...].reshape(orb, orb)
        lines = []
        for i in range(blocks):
            line = []
            for j in range(blocks):
                kept = density_ref[i, j].astype(f32)
                piece = values[i * BS:(i + 1) * BS, j * BS:(j + 1) * BS].astype(f32)
                line.append((piece * kept).astype(bf16))
            lines.append(jnp.concatenate(line, axis=1))
        full[...] = jnp.concatenate(lines, axis=0).reshape(full.shape)

    take_density(virt_all, 0)
    take_density(occ_all, 1)

    for c in range(2):
        @pl.when(core == c)
        def _():
            values = virt_all[...].reshape(orb, orb)
            right[0] = values[:, c * half:(c + 1) * half]
            right[1] = values[c * half:(c + 1) * half, :].astype(f32).T.astype(bf16)

    per = local // (quarter * cols)
    for k in range(2):
        block = 2 * x + slot(k)
        lefts[0, k * local:(k + 1) * local] = occ_all[pl.ds(block * per, per)].reshape(local, orb)
        for b in range(orb // local):
            @pl.when(block == b)
            def _():
                values = occ_all[...].reshape(orb, orb)
                lefts[1, k * local:(k + 1) * local] = (
                    values[:, b * local:(b + 1) * local].astype(f32).T.astype(bf16))

    def y_copy(d, h):
        return remote(stage.at[d, of(h)], layer.at[S + d, y, of(h)],
                      y_send.at[d, h], y_recv.at[d, h], over_row, me_col)

    def transform(d, p):
        moved = jnp.dot(whole[p].reshape(orb, orb), right[d],
                        preferred_element_type=f32).astype(bf16)
        second = jnp.dot(lefts[d], moved, preferred_element_type=f32).astype(bf16)
        layer[S + d, y, p] = second[:local]
        stage[d, p] = second[local:]

    def late(h):
        y_copy(0, h).wait_recv()

        @pl.when(z >= 2)
        def _():
            y_copy(1, h).wait_recv()
        send_z((S, T), 1, h)

    def hand_on(k, h):
        def go(sends, passed, lands):
            for i, entry in enumerate(passed):
                landing(entry[0], entry[3] + entry[4], k, h).wait_recv()
                pass_copy(i, entry, k, h).start()

        on_layer(2, go)

    lag, soon, far_lag = 7, 2, 8

    def main(h):
        gather_x(h, 1).wait_recv()
        gather_x(h, 2).start()
        gather_x(h, 0).wait_recv()
        gather_x(h, 2).wait_recv()

        def one(i):
            p = h * span + i
            transform(0, p)

            @pl.when(z >= 2)
            def _():
                transform(1, p)

        each(span, one)
        y_copy(0, h).start()

        @pl.when(z >= 2)
        def _():
            y_copy(1, h).start()
        send_z((S, T), 0, h)
        over(h, 0).wait_recv()
        send_z((X,), 1, h)

        @pl.when((y == core) & (h >= lag))
        def _():
            late(h - lag)

        @pl.when((y != core) & (h >= soon))
        def _():
            late(h - soon)

        @pl.when(h >= 1)
        def _():
            hand_on(0, h - 1)

        @pl.when(h >= far_lag)
        def _():
            hand_on(1, h - far_lag)

    each(chunks, main)

    each(1, lambda i: hand_on(0, chunks - 1 + i))
    each(far_lag, lambda i: hand_on(1, chunks - far_lag + i))

    @pl.when(y == core)
    def _():
        each(lag, lambda i: late(chunks - lag + i))

    @pl.when(y != core)
    def _():
        each(soon, lambda i: late(chunks - soon + i))

    def settle(w, slots):
        def go(sends, passed, lands):
            def one(h):
                for at, count in lands[w]:
                    if at in slots:
                        for k in range(2):
                            landing(at, count, k, h).wait_recv()
            each(chunks, one)

        on_layer(w, go)

    direct_sum[...] = jnp.zeros_like(direct_sum)
    swapped_sum[...] = jnp.zeros_like(swapped_sum)
    deep = 2 * aux
    gap = BS - 2 * deep

    def stretch(start, stop, left, rights):
        def strip(i):
            base = (start + i) * unit
            for n, (ref, shift) in enumerate([e[2:] for e in left] + [e[1:] for e in rights]):
                at = pl.ds(pl.multiple_of(base - shift * unit, unit), unit)
                for j in range(half // BS):
                    wide_rows[n, j] = ref[:, :, at, j * BS:(j + 1) * BS].astype(f32).reshape(
                        deep * unit, BS)

            def every(n, line):
                return jnp.concatenate(
                    [wide_rows[n, j, pl.ds(line, deep, stride=unit), :] for j in range(half // BS)],
                    axis=1).astype(bf16)

            chi = jnp.zeros((deep * len(left), 2 * BS), f32)
            for line in range(unit):
                lhs = jnp.concatenate([every(n, line) for n in range(len(left))], axis=0)
                have = {e[0]: len(left) + n for n, e in enumerate(rights)}
                pieces = [every(have[w], line) if w in have else jnp.zeros((deep, half), bf16)
                          for w in range(4)]
                empty = [jnp.zeros((gap, half), bf16)]
                rhs = jnp.concatenate(pieces[:2] + empty + pieces[2:] + empty, axis=0)
                chi = chi + lax.dot_general(lhs, rhs, (((1,), (1,)), ((), ())),
                                            preferred_element_type=f32)
            for n, e in enumerate(left):
                into = direct_sum if e[0] == S else swapped_sum
                at = e[1] * deep + gap * (e[1] // 2)
                into[at:at + deep] += chi[n * deep:(n + 1) * deep]

        each(stop - start, strip)

    mine_x, mine_s, mine_t = (layer.at[array] for array in range(3))

    @pl.when(z == 0)
    def _():
        settle(0, (0, 1))
        stretch(0, 5, [(S, 0, mine_s, 0), (S, 1, hub.at[1], 0)],
                [(0, mine_x, 0), (1, hub.at[0], 0)])

    @pl.when(z == 1)
    def _():
        rights = [(1, mine_x, 0), (0, hub.at[0], 5)]
        settle(1, (0, 1))
        stretch(5, 8, [(S, 1, mine_s, 0), (S, 0, hub.at[1], 5)], rights)
        settle(1, (2, 3, 4, 5))
        stretch(far_end, 8, [(S, 2, hub.at[2], far_end), (S, 3, hub.at[3], far_end),
                             (T, 2, hub.at[4], far_end), (T, 3, hub.at[5], far_end)], rights)

    @pl.when(z == 2)
    def _():
        rights = [(2, mine_x, 0), (0, hub.at[0], 0), (1, hub.at[1], 0)]
        inner = [(S, 2, mine_s, 0), (T, 2, mine_t, 0)]
        stretch(far_end, 8, inner[:1], rights[:1])
        stretch(0, far_end, inner, rights)
        settle(2, (2, 3))
        stretch(0, near_end, [(S, 3, hub.at[2], 0), (T, 3, hub.at[3], 0)], rights)

    @pl.when(z == 3)
    def _():
        inner = [(S, 3, mine_s, 0), (T, 3, mine_t, 0)]
        near = [(3, mine_x, 0), (2, hub.at[2], near_end)]
        stretch(0, near_end, inner[:1], near[:1])
        settle(3, (2,))
        stretch(near_end, 8, inner, near)
        settle(3, (0, 1))
        stretch(near_end, far_end, inner, [(0, hub.at[0], near_end), (1, hub.at[1], near_end)])

    shape = direct_sum.shape
    down, along = (lax.broadcasted_iota(jnp.int32, shape, d) for d in range(2))
    down = jnp.where(down < BS, down // deep, 2 + (down - BS) // deep)
    along = jnp.where(along < BS, along // deep, 2 + (along - BS) // deep)
    straight = (along <= down) | ((along < 2) & (down < 2))
    turned = (along < down) & (down >= 2)
    value = jnp.where(straight, direct_sum[...], 0.0)
    value = value + jnp.where(turned, swapped_sum[...], 0.0).T
    for g in range(rows):
        at = g * aux + gap * (g // (rows // 2))
        part[g] = value[at:at + aux]

    upper = me_row // (rows // 2)

    def columns(c):
        return pl.ds(pl.multiple_of(c * BS, BS), BS)

    copies = []
    for k in row_steps:
        to_row = partner(me_row, k, rows)[0]
        if k < rows // 2:
            source, target = part.at[to_row], landed.at[k]
        else:
            source, target = part.at[to_row, :, columns(upper)], landed.at[k, :, columns(upper)]
        copies.append((k, remote(source, target, row_send.at[k], row_recv.at[k], to_row, me_col)))
    for _, copy in copies:
        copy.start()
    value = part[me_row]
    across = jnp.zeros((aux, BS), f32)
    for k, copy in copies:
        copy.wait()
    for k, _ in copies:
        if k < rows // 2:
            value = value + landed[k]
        else:
            across = across + landed[k, :, columns(1 - upper)]
    value = value + jnp.concatenate(
        [jnp.where(upper == 1, across, 0.0), jnp.where(upper == 0, across, 0.0)], axis=1)
    total[...] = value
    copies = []
    for k in range(1, cols):
        to_col = partner(me_col, k, cols)[0]
        copies.append(remote(total, others.at[me_col],
                             col_send.at[k], col_recv.at[k], me_row, to_col))
    for copy in copies:
        copy.start()
    others[me_col] = value
    for copy in copies:
        copy.wait()
    value = others[0]
    for k in range(1, cols):
        value = value + others[k]
    out_ref[:, 0:2 * deep] = value[:, 0:2 * deep]
    out_ref[:, 2 * deep:4 * deep] = value[:, BS:BS + 2 * deep]

    def drain(h):
        @pl.when(y == core)
        def _():
            to_mate(h).wait_send()

        @pl.when(y != core)
        def _():
            over(h, 0).wait_send()
            over(h, 1).wait_send()
        for which in range(3):
            gather_x(h, which).wait_send()
        y_copy(0, h).wait_send()

        @pl.when(z >= 2)
        def _():
            y_copy(1, h).wait_send()
        for w in range(4):
            def go(sends, passed, lands):
                for k in range(2):
                    for i, entry in enumerate(sends[w]):
                        z_copy(i, entry, k, h).wait_send()
                    if w == 2:
                        for i, entry in enumerate(passed):
                            pass_copy(i, entry, k, h).wait_send()

            on_layer(w, go)

    each(chunks, drain)


def layered(rows, cols, three_centre, tensor_pattern, occ_density, virt_density, density_pattern):
    aux, local, orb = three_centre.shape
    quarter = occ_density.shape[0] // cols
    half, unit, total = orb // 2, local // 8, rows * aux
    bf16, f32 = jnp.bfloat16, jnp.float32
    chunks = aux // 2
    dma = pltpu.SemaphoreType.DMA
    vmem = pl.BlockSpec(memory_space=pltpu.VMEM)
    smem = pl.BlockSpec(memory_space=pltpu.SMEM)
    hbm = pl.BlockSpec(memory_space=pltpu.MemorySpace.HBM)
    return pl.pallas_call(
        functools.partial(layered_kernel, rows, cols, chunks),
        out_shape=jax.ShapeDtypeStruct((aux, total), f32),
        in_specs=[hbm, smem, hbm, hbm, smem],
        out_specs=vmem,
        scratch_shapes=[
            pltpu.VMEM((aux, cols, local, orb), bf16),
            pltpu.VMEM((3, 2, aux, local, half), bf16),
            pltpu.VMEM((2, aux, local, half), bf16),
            pltpu.VMEM((6, 2, aux, 6 * unit, half), bf16),
            pltpu.VMEM((8, half // BS, 2 * aux * unit, BS), f32),
            pltpu.VMEM((2 * BS, 2 * BS), f32),
            pltpu.VMEM((2 * BS, 2 * BS), f32),
            pltpu.VMEM((rows, aux, 2 * BS), f32),
            pltpu.VMEM((rows, aux, 2 * BS), f32),
            pltpu.VMEM((aux, 2 * BS), f32),
            pltpu.VMEM((cols, aux, 2 * BS), f32),
            pltpu.VMEM((rows, cols, quarter, orb), bf16),
            pltpu.VMEM((rows, cols, quarter, orb), bf16),
            pltpu.VMEM((2, orb, half), bf16),
            pltpu.VMEM((2, 2 * local, orb), bf16),
            dma((chunks,)), dma((2 + chunks,)),
            dma((2, rows)), dma((2, rows)), dma((2, 3)), dma((2, 3)),
            dma((2, chunks)), dma((2, chunks)), dma((3, chunks)), dma((3, chunks)),
            dma((2, chunks)), dma((2, chunks)), dma((4, 2, chunks)), dma((6, 2, chunks)),
            dma((2, 2, chunks)), dma((rows,)), dma((rows,)), dma((cols,)), dma((cols,)),
        ],
        compiler_params=pltpu.CompilerParams(
            collective_id=1, has_side_effects=True, vmem_limit_bytes=67_000_000),
    )(three_centre, tensor_pattern.transpose(1, 2, 0), occ_density, virt_density,
      density_pattern)


def staged(three_centre, tensor_pattern, occ_density, virt_density, density_pattern):
    aux_count = three_centre.shape[0]
    local_rows = three_centre.shape[1]
    orbital_count = three_centre.shape[2]
    offset = lax.axis_index("col") * local_rows
    row_blocks = (offset + jnp.arange(local_rows, dtype=jnp.int32)) // BS
    pattern_rows = jnp.take(tensor_pattern, row_blocks, axis=1)
    tensor_mask = jnp.repeat(pattern_rows, BS, 2).astype(jnp.bfloat16)
    masked = three_centre * tensor_mask
    occupied_full, virtual_full = (
        lax.all_gather(occ_density, "row", axis=0, tiled=True),
        lax.all_gather(virt_density, "row", axis=0, tiled=True),
    )
    density_mask = expand_blocks(density_pattern, BS, 0, 1).astype(jnp.bfloat16)
    occupied = occupied_full * density_mask
    virtual = virtual_full * density_mask
    moved = jnp.dot(
        masked.reshape(aux_count * local_rows, orbital_count),
        virtual,
        preferred_element_type=jnp.float32,
    ).astype(jnp.bfloat16)
    moved = moved.reshape(aux_count, local_rows, orbital_count)
    moved_cols, regrouped = (
        lax.all_to_all(moved, "col", split_axis=2, concat_axis=1, tiled=True),
        lax.all_to_all(masked, "col", split_axis=2, concat_axis=1, tiled=True),
    )
    second = jnp.einsum(
        "lm,pms->pls", occupied, moved_cols, preferred_element_type=jnp.float32
    ).astype(jnp.bfloat16)
    grouped_left, grouped_right = (
        lax.all_to_all(second, "row", split_axis=1, concat_axis=0, tiled=True),
        lax.all_to_all(regrouped, "row", split_axis=1, concat_axis=0, tiled=True),
    )
    total_aux = grouped_left.shape[0]
    left_flat = grouped_left.reshape(total_aux, -1)
    right_flat = grouped_right.reshape(total_aux, -1)
    partial_chi = lax.dot_general(
        left_flat, right_flat, (((1,), (1,)), ((), ())), preferred_element_type=jnp.float32
    )
    row_summed = lax.psum_scatter(partial_chi, "row", scatter_dimension=0, tiled=True)
    return lax.psum(row_summed, "col")


def solution(mesh):
    rows, cols = mesh.shape["row"], mesh.shape["col"]

    def per_device(three_centre, tensor_pattern, occ_density, virt_density, density_pattern):
        aux, local, orb = three_centre.shape
        aligned = (
            local % (16 * rows) == 0 and occ_density.shape[0] % (16 * cols) == 0
            and orb % (128 * cols) == 0 and BS % local == 0 and aux % 8 == 0
        )
        args = (three_centre, tensor_pattern, occ_density, virt_density, density_pattern)
        if (aligned and rows == 8 and cols == 4 and local == BS and orb == cols * local
                and 4 * aux <= BS):
            return layered(rows, cols, *args)
        return direct(rows, cols, *args) if aligned else staged(*args)

    in_specs = (P("row", "col", None), P("row", None, None), P("row", None), P("row", None), P())
    out_specs = P("row", None)
    return jax.shard_map(
        per_device, mesh=mesh, in_specs=in_specs, out_specs=out_specs, check_vma=False
    )
```
